32 devices in a mesh: occ: 8 (over z, y), vir: 4 (over x, core).
Axes of the slice: x: 2, y: 2, z: 4, core: 2. Of those that a mesh axis runs over, the one named last changes fastest.
Arguments:
- amplitudes: bfloat16 [16384, 8192], P('occ', 'vir'), may hold values from -6 to 6
- integrals: bfloat16 [8192, 8192], P('occ', 'vir'), may hold values from -0.0625 to 0.0625
- other_terms: bfloat16 [16384, 8192], P('occ', 'vir'), may hold values from -6 to 6
- occ_irrep: int32 [4], replicated, may hold values from 0 to 3, as said below
- vir_irrep: int32 [32], replicated, may hold values from 0 to 3
- pair_tiles: int32 [8, 2], replicated, may hold values from 0 to 31
- spin_mask: int32 [16, 8], replicated, may hold values 0 or 1
- occ_energy: float32 [128], replicated, may hold values from -2 to -0.5
- vir_energy: float32 [1024], replicated, may hold values from 0.2 to 3
Outputs:
- updated: bfloat16 [16384, 8192], P('occ', 'vir')
The draws below stay inside these ranges and needn't reach their ends.
Inputs may be any that keep to these rules, and one draw needn't show every extreme that they name: `occ_irrep`: the labels are not all equal. `pair_tiles`: tiles of one pair may repeat across pairs.
All inputs are finite; a program needn't handle non-finite values.
Results may differ from the reference program's by a relative error of at most 0.001.
Values may be sent and summed in bfloat16 or wider, within the bound.
A program may use at most 448 MiB of HBM per device.

```python
import jax
import jax.numpy as jnp
from jax import lax

OCC = 128
VIR = 1024
TILE = 32
NPAIR = 8
IRREPS = 4
OTILES = 4
VTILES = 32
OPAIRS = 16384
VPAIRS = 8192


def draw_occ_irrep(key, part):
    first_key = jax.random.fold_in(key, 11)
    second_key = jax.random.fold_in(key, 23)
    labels = jax.random.randint(first_key, (OTILES,), 0, IRREPS).astype(jnp.int32)
    offset = jax.random.randint(second_key, (), 1, IRREPS).astype(jnp.int32)
    return labels.at[1].set(jnp.bitwise_xor(labels[0], offset))


def touch_ends(values, own_key, smallest, high):
    longest = values.shape.index(max(values.shape))
    spots = []
    for shift in (0, 1):
        where = [jax.random.randint(jax.random.fold_in(own_key, axis), (), 0, length) for axis, length in enumerate(values.shape)]
        where[longest] = (where[longest] + shift) % values.shape[longest]
        spots.append(tuple(where))
    return values.at[spots[0]].set(smallest).at[spots[1]].set(high)


def block_levels(rng, extent, split, low, high):
    factor_of = 1.0
    for position, blocks in split:
        draws = jax.random.uniform(jax.random.fold_in(jax.random.fold_in(rng, 6), position), (blocks,), jnp.float32, low / len(split), high / len(split))
        factor_of = factor_of * jnp.repeat(jnp.exp(draws), extent[position] // blocks).reshape((-1,) + (1,) * (len(extent) - 1 - position))
    return factor_of


def gaussian(own_key, extent, width, bound, split=(), kind=jnp.bfloat16):
    level = block_levels(own_key, extent, split, -0.22, 0.18) if split else 1.0
    entries = jax.random.normal(own_key, extent, jnp.float32) * width * level
    return jnp.minimum(jnp.maximum(entries, -bound), bound).astype(kind)


def setup_inputs(seed: int = 0) -> dict:
    seeds = jax.random.split(jax.random.key(seed), 10)
    return {
        "amplitudes": gaussian(seeds[0], (OPAIRS, VPAIRS), 1.0, 6.0, ((0, 8), (1, 4))),
        "integrals": gaussian(seeds[1], (VPAIRS, VPAIRS), VPAIRS ** -0.5, 0.0625, ((0, 8), (1, 4))),
        "other_terms": gaussian(seeds[2], (OPAIRS, VPAIRS), 1.0, 6.0, ((0, 8), (1, 4))),
        "occ_irrep": draw_occ_irrep(jax.random.fold_in(seeds[9], 71), 0),
        "vir_irrep": touch_ends(jax.random.randint(seeds[4], (VTILES,), 0, IRREPS), jax.random.fold_in(seeds[4], 1), 0, IRREPS - 1).astype(jnp.int32),
        "pair_tiles": touch_ends(jax.random.randint(seeds[5], (NPAIR, 2), 0, VTILES), jax.random.fold_in(seeds[5], 1), 0, VTILES - 1).astype(jnp.int32),
        "spin_mask": touch_ends((jax.random.randint(seeds[6], (OTILES * OTILES, NPAIR), 0, 4) < 3).astype(jnp.int32), jax.random.fold_in(seeds[6], 1), 0, 1),
        "occ_energy": jnp.clip(jax.random.uniform(seeds[7], (OCC,), jnp.float32, -2.0, -0.5), -2.0, -0.5),
        "vir_energy": jnp.clip(jax.random.uniform(seeds[8], (VIR,), jnp.float32, 0.2, 3.0), 0.2, 3.0),
    }


def lookup(index, table):
    hits = index[:, None] == jnp.arange(table.shape[0], dtype=jnp.int32)[None, :]
    return jnp.sum(jnp.where(hits[:, :, None], table[None, :, :], jnp.zeros_like(table)[None, :, :]), axis=1)


def symmetry(occ_irrep, vir_irrep, pair_tiles, spin_mask):
    first = lookup(pair_tiles[:, 0], vir_irrep[:, None])[:, 0]
    second = lookup(pair_tiles[:, 1], vir_irrep[:, None])[:, 0]
    pair_irrep = jnp.bitwise_xor(first, second)
    occ_pair = jnp.bitwise_xor(occ_irrep[:, None], occ_irrep[None, :]).reshape(-1)
    allowed = jnp.where((occ_pair[:, None] == pair_irrep[None, :]) & (spin_mask == 1), 1.0, 0.0).astype(jnp.float32)
    coupled = jnp.where(pair_irrep[:, None] == pair_irrep[None, :], 1.0, 0.0).astype(jnp.float32)
    return allowed, coupled


def reference(amplitudes, integrals, other_terms, occ_irrep, vir_irrep, pair_tiles, spin_mask, occ_energy, vir_energy):
    allowed, coupled = symmetry(occ_irrep, vir_irrep, pair_tiles, spin_mask)
    square = TILE * TILE
    occ_blocks = OTILES * OTILES
    amp_four = amplitudes.reshape(occ_blocks, square, NPAIR, square)
    masked_amp = jnp.where(allowed[:, None, :, None] > 0.5, amp_four, jnp.zeros_like(amp_four)).reshape(OPAIRS, VPAIRS)
    int_four = integrals.reshape(NPAIR, square, NPAIR, square)
    masked_int = jnp.where(coupled[:, None, :, None] > 0.5, int_four, jnp.zeros_like(int_four)).reshape(VPAIRS, VPAIRS)
    height = min(512, OPAIRS)
    stacked = masked_amp.reshape(OPAIRS // height, height, VPAIRS)
    ladder = lax.map(lambda rows_block: jnp.dot(rows_block, masked_int, preferred_element_type=jnp.float32), stacked)
    ladder = ladder.reshape(occ_blocks, square, NPAIR, square)
    occ_tiles = occ_energy.reshape(OTILES, TILE)
    pair_occ = (occ_tiles[:, None, :, None] + occ_tiles[None, :, None, :]).reshape(occ_blocks, square)
    vir_tiles = vir_energy.reshape(VTILES, TILE)
    first = lookup(pair_tiles[:, 0], vir_tiles)
    second = lookup(pair_tiles[:, 1], vir_tiles)
    pair_vir = (first[:, :, None] + second[:, None, :]).reshape(NPAIR, square)
    denom = pair_occ[:, :, None, None] - pair_vir[None, None, :, :]
    other = other_terms.astype(jnp.float32).reshape(occ_blocks, square, NPAIR, square)
    updated = allowed[:, None, :, None] * ((ladder + other) / denom)
    return updated.astype(jnp.bfloat16).reshape(OPAIRS, VPAIRS)
```

```python
import functools

import jax
import jax.numpy as jnp
from jax import lax
from jax.experimental import pallas as pl
from jax.experimental.pallas import tpu as pltpu
from jax.sharding import PartitionSpec as P

TILE = 32
OTILES = 4
SQUARE = TILE * TILE
STEP_COLS = 256


def lookup(index, table):
    hits = index[:, None] == jnp.arange(table.shape[0], dtype=jnp.int32)[None, :]
    return jnp.sum(
        jnp.where(hits[:, :, None], table[None, :, :], jnp.zeros_like(table)[None, :, :]), axis=1
    )


def symmetry(occ_irrep, vir_irrep, pair_tiles, spin_mask):
    first = lookup(pair_tiles[:, 0], vir_irrep[:, None])[:, 0]
    second = lookup(pair_tiles[:, 1], vir_irrep[:, None])[:, 0]
    pair_irrep = jnp.bitwise_xor(first, second)
    occ_pair = jnp.bitwise_xor(occ_irrep[:, None], occ_irrep[None, :]).reshape(-1)
    allowed = jnp.where(
        (occ_pair[:, None] == pair_irrep[None, :]) & (spin_mask == 1), 1.0, 0.0
    ).astype(jnp.float32)
    coupled = jnp.where(pair_irrep[:, None] == pair_irrep[None, :], 1.0, 0.0).astype(jnp.float32)
    return (allowed, coupled)


def dense_device(
    amplitudes,
    integrals,
    other_terms,
    occ_irrep,
    vir_irrep,
    pair_tiles,
    spin_mask,
    occ_energy,
    vir_energy,
):
    allowed, coupled = symmetry(occ_irrep, vir_irrep, pair_tiles, spin_mask)
    height = amplitudes.shape[0]
    width = amplitudes.shape[1]
    slab_height = integrals.shape[0]
    row_global = lax.axis_index("occ") * height + jnp.arange(height, dtype=jnp.int32)
    col_global = lax.axis_index("vir") * width + jnp.arange(width, dtype=jnp.int32)
    row_block = row_global // SQUARE
    col_pair = col_global // SQUARE
    row_allowed = lookup(row_block, allowed)
    amp_keep = lookup(col_pair, row_allowed.T).T
    masked_amp = jnp.where(amp_keep > 0.5, amplitudes, jnp.zeros_like(amplitudes))
    slab_pair = (
        lax.axis_index("occ") * slab_height + jnp.arange(slab_height, dtype=jnp.int32)
    ) // SQUARE
    int_keep = lookup(col_pair, lookup(slab_pair, coupled).T).T
    masked_slab = jnp.where(int_keep > 0.5, integrals, jnp.zeros_like(integrals))
    whole_amp = lax.all_gather(masked_amp, "vir", axis=1, tiled=True)
    whole_slab = lax.all_gather(masked_slab, "occ", axis=0, tiled=True)
    ladder = jnp.dot(whole_amp, whole_slab, preferred_element_type=jnp.float32)
    inner = row_global % SQUARE
    occ_first = row_block // OTILES * TILE + inner // TILE
    occ_second = row_block % OTILES * TILE + inner % TILE
    occ_sum = (
        lookup(occ_first, occ_energy[:, None])[:, 0] + lookup(occ_second, occ_energy[:, None])[:, 0]
    )
    col_inner = col_global % SQUARE
    tile_first = lookup(col_pair, pair_tiles[:, 0:1])[:, 0]
    tile_second = lookup(col_pair, pair_tiles[:, 1:2])[:, 0]
    vir_first = tile_first * TILE + col_inner // TILE
    vir_second = tile_second * TILE + col_inner % TILE
    vir_sum = (
        lookup(vir_first, vir_energy[:, None])[:, 0] + lookup(vir_second, vir_energy[:, None])[:, 0]
    )
    denom = occ_sum[:, None] - vir_sum[None, :]
    updated = amp_keep * ((ladder + other_terms.astype(jnp.float32)) / denom)
    return updated.astype(jnp.bfloat16)


RING = 8
CHIP_BLOCKS = 4
PIECE = 32
PER_SIDE = SQUARE // 4 // PIECE
SPAN = 256
LANES = 128
LAG = 3
CHUNK = PER_SIDE
SLOTS = 8
STEPS = (40, 52, 60, 68, 76, 84, 92, 100, 108, 116, 128, 140, 156, 176, 204, 248)
WIDE_FROM = len(STEPS)
WIDE_STEPS = (128, 176, 248)
MESH = pl.DeviceIdType.MESH
SMEM_SPEC = pl.BlockSpec(memory_space=pltpu.SMEM)
VMEM_SPEC = pl.BlockSpec(memory_space=pltpu.VMEM)
ANY_SPEC = pl.BlockSpec(memory_space=pl.ANY)
ROW_AT = 0
SENT_AT = 16
VARIANT_AT = 24
SLOT_AT = 25
WIDE_AT = 27
INFO = 32


def ring_place(pos):
    late = pos // (RING // 2)
    return 2 * pos * (1 - late) + (2 * (RING - 1 - pos) + 1) * late


def ring_pos(o):
    odd = o % 2
    return (o // 2) * (1 - odd) + (RING - 1 - o // 2) * odd


def plan_kernel(occ_ref, vir_ref, pairs_ref, spin_ref, inject_ref, when_ref, info_ref):
    o = lax.axis_index("occ")
    v = lax.axis_index("vir")
    one = jnp.int32(1)

    def flag(condition):
        return jnp.where(condition, one, 0)

    pair = [vir_ref[pairs_ref[t, 0]] ^ vir_ref[pairs_ref[t, 1]] for t in range(8)]
    rows, spread = [], []
    for q in range(16):
        own = occ_ref[q // OTILES] ^ occ_ref[q % OTILES]
        row, wide_row = jnp.int32(0), jnp.int32(0)
        for t in range(8):
            hit = flag((own == pair[t]) & (spin_ref[q, t] == 1))
            row = row | (hit << t)
            wide_row = wide_row | (hit << (4 * t))
        rows.append(row)
        spread.append(wide_row)
        info_ref[ROW_AT + q] = row
    far = [[], []]
    for s in range(8):
        at_pos = {}
        for chip in range(8):
            at_pos[ring_pos(chip)] = (spread[2 * chip] * ((rows[2 * chip] >> s) & 1)) | (
                spread[2 * chip + 1] * ((rows[2 * chip + 1] >> s) & 1)
            )
        for side in range(2):
            reach = jnp.int32(0)
            for away in range(1, RING):
                there = at_pos[(ring_pos(s) + (away if side == 0 else -away)) % RING]
                reach = (reach & ~(there * 15)) | (there * away)
            far[side].append(reach)
        sent = jnp.int32(0)
        for t in range(8):
            sent = sent | (flag(((far[0][s] >> (4 * t)) & 15) > 0) << t)
        info_ref[SENT_AT + s] = sent

    most = jnp.int32(0)
    for p in range(8):
        both = [rows[2 * p] , rows[2 * p + 1]]
        for w in range(4):
            bits = [(row >> (2 * w + k)) & 1 for row in both for k in range(2)]
            most = jnp.maximum(most, bits[0] + bits[1] + bits[2] + bits[3])
    mine = [info_ref[ROW_AT + 2 * o + r] for r in range(2)]
    rank = jnp.int32(0)
    picks = [jnp.int32(0), jnp.int32(0)]
    for k in range(4):
        bit = (mine[k // 2] >> (2 * v + k % 2)) & 1
        picks = [jnp.where((bit == 1) & (rank == j), k, picks[j]) for j in range(2)]
        rank = rank + bit
    for j in range(2):
        info_ref[SLOT_AT + j] = picks[j]
    wide = flag(most > 2)
    info_ref[WIDE_AT] = wide

    shape = (RING, LANES)
    at = lax.broadcasted_iota(jnp.int32, shape, 0)
    lane = lax.broadcasted_iota(jnp.int32, shape, 1)
    zero = jnp.minimum(at + lane, 0)
    totals, lists, travels = [], [], []
    bound = jnp.int32(0)
    for plane in range(2):
        total, listed = zero, zero
        travel = [zero, zero]
        whole = jnp.int32(0)
        for s in range(8):
            rank = jnp.int32(0)
            order = jnp.int32(0)
            hops = [jnp.int32(0), jnp.int32(0)]
            for k in range(CHIP_BLOCKS):
                reach = [(far[side][s] >> (4 * (CHIP_BLOCKS * plane + k))) & 15 for side in range(2)]
                bit = flag(reach[0] > 0)
                order = order | ((bit * k) << (2 * rank))
                hops = [hops[side] | (reach[side] << (4 * rank)) for side in range(2)]
                rank = rank + bit
            here = at == ring_pos(s)
            total = jnp.where(here, rank, total)
            listed = jnp.where(here, order, listed)
            travel = [jnp.where(here, hops[side], travel[side]) for side in range(2)]
            whole = whole + rank
        bound = jnp.maximum(bound, whole)
        totals.append(total)
        lists.append(listed)
        travels.append(travel)

    sims = [(plane, side) for plane in range(2) for side in range(2)]

    def big_step(turn, carry):
        out = []
        for (plane, side), (passing, counts, when, inject) in zip(sims, carry):
            counts = list(counts)
            word = zero
            for p in range(PER_SIDE):
                arrived = pltpu.roll(passing[0], 1 if side == 0 else RING - 1, 0)
                arrived = jnp.maximum(arrived - 1, 0)
                count = counts[p]
                starts = (arrived == 0) & (count < totals[plane])
                hops = (travels[plane][side] >> (4 * count)) & 15
                block = (lists[plane] >> (2 * count)) & 3
                passing = passing[1:] + (jnp.where(starts, hops, arrived),)
                now = turn * PER_SIDE + p
                when = jnp.where(starts & (lane == count * PER_SIDE + p), now, when)
                word = word | (jnp.where(starts, block + 1, 0) << (4 * p))
                counts[p] = jnp.where(starts, count + 1, count)
            inject = jnp.where(lane == turn, word, inject)
            out.append((passing, tuple(counts), when, inject))
        return tuple(out)

    first = tuple(((zero,) * LAG, (zero,) * PER_SIDE, zero, zero) for _ in sims)
    done = lax.fori_loop(0, bound, big_step, first)
    last = zero
    chip_plane = v // 2
    for side in range(2):
        when_ref[side] = jnp.where(chip_plane == 0, done[side][2], done[2 + side][2])
        inject_ref[side] = jnp.where(chip_plane == 0, done[side][3], done[2 + side][3])
    rank = jnp.minimum(lane // PER_SIDE, CHIP_BLOCKS)
    for (plane, side), state in zip(sims, done):
        hops = (travels[plane][side] >> (4 * rank)) & 15
        last = jnp.maximum(last, jnp.where(rank < totals[plane], state[2] + LAG * (hops - 1), 0))
    need = jnp.max(last) + 1
    variant = jnp.int32(0)
    for steps in STEPS[:-1]:
        variant = variant + flag(need > steps)
    wide_variant = jnp.int32(WIDE_FROM)
    for steps in WIDE_STEPS[:-1]:
        wide_variant = wide_variant + flag(need > steps)
    info_ref[VARIANT_AT] = jnp.where(wide == 1, wide_variant, variant)


def plan(occ_irrep, vir_irrep, pair_tiles, spin_mask):
    table = jax.ShapeDtypeStruct((2, RING, LANES), jnp.int32)
    return pl.pallas_call(
        plan_kernel,
        out_shape=(table, table, jax.ShapeDtypeStruct((INFO,), jnp.int32)),
        in_specs=[SMEM_SPEC] * 4,
        out_specs=(VMEM_SPEC, VMEM_SPEC, SMEM_SPEC),
        name="plan",
    )(occ_irrep, vir_irrep, pair_tiles, spin_mask)


def ring_kernel(
    steps,
    cap,
    inject_ref,
    info_ref,
    amp_ref,
    int_ref,
    a_ref,
    b_ref,
    own,
    land,
    leave,
    *rest,
):
    if cap == 2:
        amp_own, amp_out = rest[:2]
        rest = rest[2:]
        amp_in = rest[0]
        rest = rest[1:]
    own_in, own_send, own_recv, send, recv, kept, f_send, f_recv, a_send, a_recv = rest
    o = lax.axis_index("occ")
    v = lax.axis_index("vir")
    core = v % 2
    mate = v + 1 - 2 * core
    across = (v + 2) % 4
    pos = ring_pos(o)
    right = ring_place((pos + 1) % RING)
    left = ring_place((pos + RING - 1) % RING)
    half = SQUARE // 2

    def own_copy(k):
        return pltpu.make_async_copy(
            int_ref.at[pl.ds(core * half, half), pl.ds(k * SQUARE, SQUARE)],
            own.at[pl.ds((2 * core + k) * half, half)],
            own_in.at[k],
        )

    def own_remote(k):
        return pltpu.make_async_remote_copy(
            src_ref=int_ref.at[pl.ds((1 - core) * half, half), pl.ds(k * SQUARE, SQUARE)],
            dst_ref=own.at[pl.ds((2 * core + k) * half, half)],
            send_sem=own_send.at[k],
            recv_sem=own_recv.at[k],
            device_id=(o, mate),
            device_id_type=MESH,
        )

    def amp_copy(k):
        return pltpu.make_async_copy(
            amp_ref.at[pl.ds(k // 2 * SQUARE, SQUARE), pl.ds(k % 2 * SQUARE, SQUARE)],
            amp_own.at[k],
            amp_in.at[k],
        )

    for k in range(2):
        own_copy(k).start()
    if cap == 2:
        for k in range(4):
            amp_copy(k).start()

    barrier = pltpu.get_barrier_semaphore()
    for target in ((right, v), (left, v), (o, mate), (o, across)):
        pl.semaphore_signal(barrier, inc=1, device_id=target, device_id_type=MESH)
    pl.semaphore_wait(barrier, 4)

    for k in range(2):
        own_remote(k).start()

    def a_copy(which, slot, owner, target):
        if which == 2:
            source = a_ref.at[owner, slot]
        elif cap == 2:
            source = amp_out.at[slot]
        else:
            source = amp_ref.at[
                pl.ds(slot // 2 * SQUARE, SQUARE), pl.ds(slot % 2 * SQUARE, SQUARE)
            ]
        return pltpu.make_async_remote_copy(
            src_ref=source,
            dst_ref=a_ref.at[owner, slot],
            send_sem=a_send.at[which, slot],
            recv_sem=a_recv.at[which, slot],
            device_id=(o, target),
            device_id_type=MESH,
        )

    def hop(side, tau, p):
        return pltpu.make_async_remote_copy(
            src_ref=leave.at[side, p],
            dst_ref=land.at[side, tau],
            send_sem=send.at[side, p],
            recv_sem=recv.at[side, tau],
            device_id=(right if side == 0 else left, v),
            device_id_type=MESH,
        )

    def compose(side, turn, p, forward):
        tau = turn * CHUNK + p
        block = (inject_ref[side, pos, turn] >> (4 * p)) & 15
        pieces = [
            own[pl.ds((k * 2 * PER_SIDE + side * PER_SIDE + p) * PIECE, PIECE), :]
            for k in range(CHIP_BLOCKS)
        ]
        value = land[side, tau - LAG] if forward else pieces[0]
        for k in range(CHIP_BLOCKS):
            value = jnp.where(block == k + 1, pieces[k], value)
        leave[side, p] = value

    def pass_on(start, size, side):
        cut = pl.ds(start, size)
        stay = pltpu.make_async_copy(land.at[side, cut], b_ref.at[core, side, cut], kept)
        give = pltpu.make_async_remote_copy(
            src_ref=land.at[side, cut],
            dst_ref=b_ref.at[core, side, cut],
            send_sem=f_send,
            recv_sem=f_recv,
            device_id=(o, mate),
            device_id_type=MESH,
        )
        return stay, give

    def advance(turn, p, fresh):
        tau = turn * CHUNK + p
        for side in range(2):
            forward = not (fresh and p < LAG)
            if forward:
                hop(side, tau - LAG, (p - LAG) % CHUNK).wait_recv()
            if not fresh:
                hop(side, tau - SLOTS, p).wait_send()
            compose(side, turn, p, forward)
            hop(side, tau, p).start()

    for k in range(2):
        own_copy(k).wait()
    for k in range(2):
        own_remote(k).wait_recv()
    for p in range(LAG):
        advance(0, p, True)
    if cap == 2:
        for k in range(4):
            amp_copy(k).wait()
    for slot in range(cap):
        if cap == 2:
            pick = info_ref[SLOT_AT + slot]

            @pl.loop(0, SQUARE // 64)
            def _(part):
                cut = pl.ds(pl.multiple_of(part * 64, 64), 64)
                value = amp_own[0, cut]
                for k in range(1, 4):
                    value = jnp.where(pick == k, amp_own[k, cut], value)
                amp_out[slot, cut] = value

        a_copy(0, slot, v, across).start()
        a_copy(1, slot, v, mate).start()
    for p in range(LAG, CHUNK):
        advance(0, p, True)

    full = steps // CHUNK

    def hand_over(start, size):
        for side in range(2):
            for copy in pass_on(start, size, side):
                copy.start()

    @pl.loop(1, full)
    def _(turn):
        for p in range(CHUNK):
            advance(turn, p, False)
            if p == LAG - 1:
                hand_over((turn - 1) * CHUNK, CHUNK)

    for p in range(steps % CHUNK):
        advance(full, p, False)

    for slot in range(cap):
        a_copy(0, slot, v, across).wait_recv()
        a_copy(2, slot, across, mate).start()
    for tau in range(steps - LAG, steps):
        for side in range(2):
            hop(side, tau, tau % CHUNK).wait_recv()
    hand_over((full - 1) * CHUNK, CHUNK + steps % CHUNK)
    for tau in range(steps - SLOTS, steps):
        for side in range(2):
            hop(side, tau, tau % CHUNK).wait_send()
    for k in range(2):
        own_remote(k).wait_send()
    for which in range(3):
        for slot in range(cap):
            copy = a_copy(which, slot, across if which == 2 else v, across if which == 0 else mate)
            copy.wait_send()
            if which > 0:
                copy.wait_recv()
    every = pl.ds(0, steps)
    pltpu.make_async_copy(land, b_ref.at[core, :, every], kept).wait()
    total = pltpu.make_async_remote_copy(
        src_ref=land,
        dst_ref=b_ref.at[1 - core, :, every],
        send_sem=f_send,
        recv_sem=f_recv,
        device_id=(o, mate),
        device_id_type=MESH,
    )
    total.wait_send()
    total.wait_recv()


def ring(which, steps, cap, inject, info, amplitudes, integrals):
    square = (SQUARE, SQUARE)
    dma = pltpu.SemaphoreType.DMA
    kind = amplitudes.dtype
    amp_scratch = []
    if cap == 2:
        amp_scratch = [
            pltpu.VMEM((4,) + square, kind),
            pltpu.VMEM((2,) + square, kind),
            dma((4,)),
        ]
    return pl.pallas_call(
        functools.partial(ring_kernel, steps, cap),
        out_shape=(
            jax.ShapeDtypeStruct((4, 4) + square, kind),
            jax.ShapeDtypeStruct((2, 2, SPAN, PIECE, SQUARE), kind),
        ),
        in_specs=[SMEM_SPEC, SMEM_SPEC, ANY_SPEC, ANY_SPEC],
        out_specs=(ANY_SPEC, ANY_SPEC),
        scratch_shapes=[
            pltpu.VMEM((2 * SQUARE, SQUARE), kind),
            pltpu.VMEM((2, steps, PIECE, SQUARE), kind),
            pltpu.VMEM((2, SLOTS, PIECE, SQUARE), kind),
        ]
        + amp_scratch
        + [
            dma((2,)),
            dma((2,)),
            dma((2,)),
            dma((2, SLOTS)),
            dma((2, steps)),
            dma,
            dma,
            dma,
            dma((3, cap)),
            dma((3, cap)),
        ],
        compiler_params=pltpu.CompilerParams(
            collective_id=which, has_side_effects=True, vmem_limit_bytes=58 << 20
        ),
        name="ring",
    )(inject, info, amplitudes, integrals)


def ladder_kernel(
    info_ref,
    when_ref,
    occ_ref,
    vir_ref,
    amp_ref,
    int_ref,
    a_ref,
    b_ref,
    other_ref,
    out_ref,
    terms,
    a_buf,
    b_buf,
    other_buf,
    acc,
    result,
    blank,
    a_sem,
    b_sem,
    other_sem,
    out_sem,
    blank_sem,
):
    o = lax.axis_index("occ")
    v = lax.axis_index("vir")
    pos = ring_pos(o)
    wide = info_ref[WIDE_AT]
    rows = [info_ref[ROW_AT + 2 * o + r] for r in range(2)]

    def out_block(ref, b):
        return ref.at[
            pl.ds(pl.multiple_of(b // 2 * SQUARE, SQUARE), SQUARE),
            pl.ds(pl.multiple_of(b % 2 * SQUARE, SQUARE), SQUARE),
        ]

    def keep(b):
        return ((rows[b // 2] >> (2 * v + b % 2)) & 1) == 1

    count = jnp.int32(0)
    for b in range(4):
        alive = jnp.where(keep(b), 1, 0)
        for s in range(8):
            bit = alive * ((rows[b // 2] >> s) & 1)

            @pl.when(bit == 1)
            def _():
                terms[count] = b * 8 + s

            count = count + bit
    terms[count] = 64

    def fetch(j, slot):
        code = terms[j]
        b = code // 8
        s = code % 8
        r = b // 2
        tile = 2 * (v % 2) + b % 2
        src = s // 2
        block = r * 2 + s % 2

        @pl.when(src == v)
        def _():
            pltpu.make_async_copy(out_block(amp_ref, block), a_buf.at[slot], a_sem.at[slot]).start()

        @pl.when(src != v)
        def _():
            low = (rows[0] >> (2 * src)) & 3
            high = (rows[1] >> (2 * src)) & 3
            flags = low | (high << 2)
            below = flags & ((1 << block) - 1)
            rank = (below & 1) + ((below >> 1) & 1) + ((below >> 2) & 1)
            at = jnp.where(wide == 1, block, rank)
            pltpu.make_async_copy(a_ref.at[src, at], a_buf.at[slot], a_sem.at[slot]).start()

        @pl.when(s == o)
        def _():
            pltpu.make_async_copy(
                int_ref.at[:, pl.ds(pl.multiple_of(b % 2 * SQUARE, SQUARE), SQUARE)],
                b_buf.at[slot],
                b_sem.at[slot],
            ).start()

        @pl.when(s != o)
        def _():
            flags = (info_ref[SENT_AT + s] >> (CHIP_BLOCKS * (v // 2))) & 15
            below = flags & ((1 << tile) - 1)
            rank = (below & 1) + ((below >> 1) & 1) + ((below >> 2) & 1)
            owner = ring_pos(s)
            for side in range(2):
                away = (pos - owner if side == 0 else owner - pos) % RING
                for p in range(PER_SIDE):
                    start = when_ref[side, owner, rank * PER_SIDE + p]
                    step = start + LAG * (away - 1)
                    for core in range(2):
                        row = core * (SQUARE // 2) + (side * PER_SIDE + p) * PIECE
                        pltpu.make_async_copy(
                            b_ref.at[core, side, step],
                            b_buf.at[slot, pl.ds(row, PIECE)],
                            b_sem.at[slot],
                        ).start()

    @pl.when(count > 0)
    def _():
        fetch(0, 0)

    def other_copy(b):
        return pltpu.make_async_copy(out_block(other_ref, b), other_buf.at[b], other_sem.at[b])

    def blank_copy(b):
        return pltpu.make_async_copy(blank, out_block(out_ref, b), blank_sem.at[b])

    for b in range(4):

        @pl.when(keep(b))
        def _():
            other_copy(b).start()

    blank[...] = jnp.zeros_like(blank)
    for b in range(4):

        @pl.when(jnp.logical_not(keep(b)))
        def _():
            blank_copy(b).start()

    def out_copy(b):
        return pltpu.make_async_copy(result.at[b % 2], out_block(out_ref, b), out_sem.at[b % 2])

    @pl.loop(0, count, init_carry=(jnp.int32(-1), jnp.int32(-1)))
    def last_out(j, carry):
        slot = j % 2

        @pl.when(j + 1 < count)
        def _():
            fetch(j + 1, 1 - slot)

        code = terms[j]
        b = code // 8
        before = jnp.where(j == 0, -1, terms[jnp.maximum(j - 1, 0)] // 8)
        fresh = before != b
        final = terms[j + 1] // 8 != b
        pltpu.make_async_copy(out_block(amp_ref, 0), a_buf.at[slot], a_sem.at[slot]).wait()
        pltpu.make_async_copy(out_block(amp_ref, 0), b_buf.at[slot], b_sem.at[slot]).wait()

        @pl.loop(0, SQUARE // STEP_COLS)
        def _(part):
            cols = pl.ds(pl.multiple_of(part * STEP_COLS, STEP_COLS), STEP_COLS)
            term = jnp.dot(
                a_buf[slot], b_buf[slot, :, cols], preferred_element_type=jnp.float32
            )

            @pl.when(fresh)
            def _():
                acc[:, cols] = term

            @pl.when(jnp.logical_not(fresh))
            def _():
                acc[:, cols] += term

        @pl.when(final)
        def _():
            other_copy(b).wait()
            pending = jnp.where(b % 2 == 0, carry[0], carry[1])

            @pl.when(pending >= 0)
            def _():
                out_copy(b).wait()

            @pl.loop(0, SQUARE // 64)
            def _(part):
                cut = pl.ds(pl.multiple_of(part * 64, 64), 64)
                denom = occ_ref[b // 2, cut, :] - vir_ref[b % 2]
                total = acc[cut, :] + other_buf[b, cut, :].astype(jnp.float32)
                result[b % 2, cut, :] = (total / denom).astype(result.dtype)

            out_copy(b).start()

        even = jnp.where(final & (b % 2 == 0), b, carry[0])
        odd = jnp.where(final & (b % 2 == 1), b, carry[1])
        return even, odd

    for k in range(2):

        @pl.when(last_out[k] >= 0)
        def _():
            out_copy(k).wait()

    for b in range(4):

        @pl.when(jnp.logical_not(keep(b)))
        def _():
            blank_copy(b).wait()


def ladder(info, when, occ_sum, vir_sum, amplitudes, integrals, a_all, b_all, other_terms):
    square = (SQUARE, SQUARE)
    kind = amplitudes.dtype
    dma = pltpu.SemaphoreType.DMA
    return pl.pallas_call(
        ladder_kernel,
        out_shape=jax.ShapeDtypeStruct(other_terms.shape, other_terms.dtype),
        in_specs=[SMEM_SPEC, SMEM_SPEC, VMEM_SPEC, VMEM_SPEC] + [ANY_SPEC] * 5,
        out_specs=ANY_SPEC,
        scratch_shapes=[
            pltpu.SMEM((40,), jnp.int32),
            pltpu.VMEM((2,) + square, kind),
            pltpu.VMEM((2,) + square, kind),
            pltpu.VMEM((4,) + square, kind),
            pltpu.VMEM(square, jnp.float32),
            pltpu.VMEM((2,) + square, kind),
            pltpu.VMEM(square, kind),
            dma((2,)),
            dma((2,)),
            dma((4,)),
            dma((2,)),
            dma((4,)),
        ],
        compiler_params=pltpu.CompilerParams(vmem_limit_bytes=48 << 20),
        name="ladder",
    )(info, when, occ_sum, vir_sum, amplitudes, integrals, a_all, b_all, other_terms)


def block_device(
    amplitudes,
    integrals,
    other_terms,
    occ_irrep,
    vir_irrep,
    pair_tiles,
    spin_mask,
    occ_energy,
    vir_energy,
):
    o = lax.axis_index("occ")
    v = lax.axis_index("vir")
    occ_tiles = occ_energy.reshape(OTILES, TILE)
    pair_occ = (occ_tiles[:, None, :, None] + occ_tiles[None, :, None, :]).reshape(-1, SQUARE)
    occ_sum = lax.dynamic_slice_in_dim(pair_occ, 2 * o, 2, 0)[:, :, None]
    vir_tiles = vir_energy.reshape(-1, TILE)
    tiles = lax.dynamic_slice_in_dim(pair_tiles, 2 * v, 2, 0)
    first = lookup(tiles[:, 0], vir_tiles)
    second = lookup(tiles[:, 1], vir_tiles)
    vir_sum = (first[:, :, None] + second[:, None, :]).reshape(2, 1, SQUARE)

    inject, when, info = plan(occ_irrep, vir_irrep, pair_tiles, spin_mask)
    inject, when, info, occ_sum, vir_sum = lax.optimization_barrier(
        (inject, when, info, occ_sum, vir_sum)
    )
    branches = [functools.partial(ring, k, steps, 2) for k, steps in enumerate(STEPS)]
    branches += [
        functools.partial(ring, WIDE_FROM + k, steps, 4) for k, steps in enumerate(WIDE_STEPS)
    ]
    a_all, b_all = lax.switch(
        info[VARIANT_AT], branches, inject, info, amplitudes, integrals
    )
    return ladder(info, when, occ_sum, vir_sum, amplitudes, integrals, a_all, b_all, other_terms)


def per_device(amplitudes, integrals, *rest):
    blocks = amplitudes.shape == (2 * SQUARE, 2 * SQUARE)
    blocks = blocks and integrals.shape == (SQUARE, 2 * SQUARE) and lax.axis_size("vir") == 4
    blocks = blocks and lax.axis_size("occ") == OTILES * OTILES // 2
    device = block_device if blocks else dense_device
    return device(amplitudes, integrals, *rest)


def solution(mesh):
    in_specs = (P("occ", "vir"), P("occ", "vir"), P("occ", "vir"), P(), P(), P(), P(), P(), P())
    out_specs = P("occ", "vir")
    return jax.shard_map(
        per_device, mesh=mesh, in_specs=in_specs, out_specs=out_specs, check_vma=False
    )
```

```python
import functools

import jax
import jax.numpy as jnp
from jax import lax
from jax.experimental import pallas as pl
from jax.experimental.pallas import tpu as pltpu
from jax.sharding import PartitionSpec as P

TILE = 32
OTILES = 4
SQUARE = TILE * TILE
STEP_COLS = 512


def lookup(index, table):
    hits = index[:, None] == jnp.arange(table.shape[0], dtype=jnp.int32)[None, :]
    return jnp.sum(
        jnp.where(hits[:, :, None], table[None, :, :], jnp.zeros_like(table)[None, :, :]), axis=1
    )


def symmetry(occ_irrep, vir_irrep, pair_tiles, spin_mask):
    first = lookup(pair_tiles[:, 0], vir_irrep[:, None])[:, 0]
    second = lookup(pair_tiles[:, 1], vir_irrep[:, None])[:, 0]
    pair_irrep = jnp.bitwise_xor(first, second)
    occ_pair = jnp.bitwise_xor(occ_irrep[:, None], occ_irrep[None, :]).reshape(-1)
    allowed = jnp.where(
        (occ_pair[:, None] == pair_irrep[None, :]) & (spin_mask == 1), 1.0, 0.0
    ).astype(jnp.float32)
    coupled = jnp.where(pair_irrep[:, None] == pair_irrep[None, :], 1.0, 0.0).astype(jnp.float32)
    return (allowed, coupled)


def dense_device(
    amplitudes,
    integrals,
    other_terms,
    occ_irrep,
    vir_irrep,
    pair_tiles,
    spin_mask,
    occ_energy,
    vir_energy,
):
    allowed, coupled = symmetry(occ_irrep, vir_irrep, pair_tiles, spin_mask)
    height = amplitudes.shape[0]
    width = amplitudes.shape[1]
    slab_height = integrals.shape[0]
    row_global = lax.axis_index("occ") * height + jnp.arange(height, dtype=jnp.int32)
    col_global = lax.axis_index("vir") * width + jnp.arange(width, dtype=jnp.int32)
    row_block = row_global // SQUARE
    col_pair = col_global // SQUARE
    row_allowed = lookup(row_block, allowed)
    amp_keep = lookup(col_pair, row_allowed.T).T
    masked_amp = jnp.where(amp_keep > 0.5, amplitudes, jnp.zeros_like(amplitudes))
    slab_pair = (
        lax.axis_index("occ") * slab_height + jnp.arange(slab_height, dtype=jnp.int32)
    ) // SQUARE
    int_keep = lookup(col_pair, lookup(slab_pair, coupled).T).T
    masked_slab = jnp.where(int_keep > 0.5, integrals, jnp.zeros_like(integrals))
    whole_amp = lax.all_gather(masked_amp, "vir", axis=1, tiled=True)
    whole_slab = lax.all_gather(masked_slab, "occ", axis=0, tiled=True)
    ladder = jnp.dot(whole_amp, whole_slab, preferred_element_type=jnp.float32)
    inner = row_global % SQUARE
    occ_first = row_block // OTILES * TILE + inner // TILE
    occ_second = row_block % OTILES * TILE + inner % TILE
    occ_sum = (
        lookup(occ_first, occ_energy[:, None])[:, 0] + lookup(occ_second, occ_energy[:, None])[:, 0]
    )
    col_inner = col_global % SQUARE
    tile_first = lookup(col_pair, pair_tiles[:, 0:1])[:, 0]
    tile_second = lookup(col_pair, pair_tiles[:, 1:2])[:, 0]
    vir_first = tile_first * TILE + col_inner // TILE
    vir_second = tile_second * TILE + col_inner % TILE
    vir_sum = (
        lookup(vir_first, vir_energy[:, None])[:, 0] + lookup(vir_second, vir_energy[:, None])[:, 0]
    )
    denom = occ_sum[:, None] - vir_sum[None, :]
    updated = amp_keep * ((ladder + other_terms.astype(jnp.float32)) / denom)
    return updated.astype(jnp.bfloat16)


RING = 8
CHIP_BLOCKS = 4
PIECE = 32
PER_SIDE = SQUARE // 4 // PIECE
SPAN = 256
LANES = 128
LAG = 3
CHUNK = PER_SIDE
SLOTS = 8
GROUPS = 4
A_PARTS = 4
A_LATE = 3
STEPS = (40, 52, 60, 68, 76, 84, 92, 100, 108, 116, 128, 140, 156, 176, 204, 248)
WIDE_FROM = len(STEPS)
WIDE_STEPS = (128, 176, 248)
MESH = pl.DeviceIdType.MESH
SMEM_SPEC = pl.BlockSpec(memory_space=pltpu.SMEM)
VMEM_SPEC = pl.BlockSpec(memory_space=pltpu.VMEM)
ANY_SPEC = pl.BlockSpec(memory_space=pl.ANY)
ROW_AT = 0
SENT_AT = 16
VARIANT_AT = 24
SLOT_AT = 25
WIDE_AT = 27
INFO = 32


def ring_place(pos):
    late = pos // (RING // 2)
    return 2 * pos * (1 - late) + (2 * (RING - 1 - pos) + 1) * late


def ring_pos(o):
    odd = o % 2
    return (o // 2) * (1 - odd) + (RING - 1 - o // 2) * odd


def plan_kernel(occ_ref, vir_ref, pairs_ref, spin_ref, inject_ref, when_ref, info_ref):
    o = lax.axis_index("occ")
    v = lax.axis_index("vir")
    one = jnp.int32(1)

    def flag(condition):
        return jnp.where(condition, one, 0)

    pair = [vir_ref[pairs_ref[t, 0]] ^ vir_ref[pairs_ref[t, 1]] for t in range(8)]
    rows, spread = [], []
    for q in range(16):
        own = occ_ref[q // OTILES] ^ occ_ref[q % OTILES]
        row, wide_row = jnp.int32(0), jnp.int32(0)
        for t in range(8):
            hit = flag((own == pair[t]) & (spin_ref[q, t] == 1))
            row = row | (hit << t)
            wide_row = wide_row | (hit << (4 * t))
        rows.append(row)
        spread.append(wide_row)
        info_ref[ROW_AT + q] = row
    far = [[], []]
    for s in range(8):
        at_pos = {}
        for chip in range(8):
            at_pos[ring_pos(chip)] = (spread[2 * chip] * ((rows[2 * chip] >> s) & 1)) | (
                spread[2 * chip + 1] * ((rows[2 * chip + 1] >> s) & 1)
            )
        for side in range(2):
            reach = jnp.int32(0)
            for away in range(1, RING):
                there = at_pos[(ring_pos(s) + (away if side == 0 else -away)) % RING]
                reach = (reach & ~(there * 15)) | (there * away)
            far[side].append(reach)
        sent = jnp.int32(0)
        for t in range(8):
            sent = sent | (flag(((far[0][s] >> (4 * t)) & 15) > 0) << t)
        info_ref[SENT_AT + s] = sent

    most = jnp.int32(0)
    for p in range(8):
        both = [rows[2 * p] , rows[2 * p + 1]]
        for w in range(4):
            bits = [(row >> (2 * w + k)) & 1 for row in both for k in range(2)]
            most = jnp.maximum(most, bits[0] + bits[1] + bits[2] + bits[3])
    mine = [info_ref[ROW_AT + 2 * o + r] for r in range(2)]
    rank = jnp.int32(0)
    picks = [jnp.int32(0), jnp.int32(0)]
    for k in range(4):
        bit = (mine[k // 2] >> (2 * v + k % 2)) & 1
        picks = [jnp.where((bit == 1) & (rank == j), k, picks[j]) for j in range(2)]
        rank = rank + bit
    for j in range(2):
        info_ref[SLOT_AT + j] = picks[j]
    wide = flag(most > 2)
    info_ref[WIDE_AT] = wide

    shape = (RING, LANES)
    at = lax.broadcasted_iota(jnp.int32, shape, 0)
    lane = lax.broadcasted_iota(jnp.int32, shape, 1)
    zero = jnp.minimum(at + lane, 0)
    totals, lists, travels = [], [], []
    bound = jnp.int32(0)
    for plane in range(2):
        total, listed = zero, zero
        travel = [zero, zero]
        whole = jnp.int32(0)
        for s in range(8):
            rank = jnp.int32(0)
            order = jnp.int32(0)
            hops = [jnp.int32(0), jnp.int32(0)]
            for k in range(CHIP_BLOCKS):
                reach = [(far[side][s] >> (4 * (CHIP_BLOCKS * plane + k))) & 15 for side in range(2)]
                bit = flag(reach[0] > 0)
                order = order | ((bit * k) << (2 * rank))
                hops = [hops[side] | (reach[side] << (4 * rank)) for side in range(2)]
                rank = rank + bit
            here = at == ring_pos(s)
            total = jnp.where(here, rank, total)
            listed = jnp.where(here, order, listed)
            travel = [jnp.where(here, hops[side], travel[side]) for side in range(2)]
            whole = whole + rank
        bound = jnp.maximum(bound, whole)
        totals.append(total)
        lists.append(listed)
        travels.append(travel)

    sims = [(plane, side) for plane in range(2) for side in range(2)]

    def big_step(turn, carry):
        out = []
        for (plane, side), (passing, counts, when, inject) in zip(sims, carry):
            counts = list(counts)
            word = zero
            for p in range(PER_SIDE):
                arrived = pltpu.roll(passing[0], 1 if side == 0 else RING - 1, 0)
                arrived = jnp.maximum(arrived - 1, 0)
                count = counts[p]
                starts = (arrived == 0) & (count < totals[plane])
                hops = (travels[plane][side] >> (4 * count)) & 15
                block = (lists[plane] >> (2 * count)) & 3
                passing = passing[1:] + (jnp.where(starts, hops, arrived),)
                now = turn * PER_SIDE + p
                when = jnp.where(starts & (lane == count * PER_SIDE + p), now, when)
                word = word | (jnp.where(starts, block + 1, 0) << (4 * p))
                counts[p] = jnp.where(starts, count + 1, count)
            inject = jnp.where(lane == turn, word, inject)
            out.append((passing, tuple(counts), when, inject))
        return tuple(out)

    first = tuple(((zero,) * LAG, (zero,) * PER_SIDE, zero, zero) for _ in sims)
    done = lax.fori_loop(0, bound, big_step, first)
    last = zero
    chip_plane = v // 2
    for side in range(2):
        when_ref[side] = jnp.where(chip_plane == 0, done[side][2], done[2 + side][2])
        inject_ref[side] = jnp.where(chip_plane == 0, done[side][3], done[2 + side][3])
    rank = jnp.minimum(lane // PER_SIDE, CHIP_BLOCKS)
    for (plane, side), state in zip(sims, done):
        hops = (travels[plane][side] >> (4 * rank)) & 15
        last = jnp.maximum(last, jnp.where(rank < totals[plane], state[2] + LAG * (hops - 1), 0))
    need = jnp.max(last) + 1
    variant = jnp.int32(0)
    for steps in STEPS[:-1]:
        variant = variant + flag(need > steps)
    wide_variant = jnp.int32(WIDE_FROM)
    for steps in WIDE_STEPS[:-1]:
        wide_variant = wide_variant + flag(need > steps)
    info_ref[VARIANT_AT] = jnp.where(wide == 1, wide_variant, variant)


def plan(occ_irrep, vir_irrep, pair_tiles, spin_mask):
    table = jax.ShapeDtypeStruct((2, RING, LANES), jnp.int32)
    return pl.pallas_call(
        plan_kernel,
        out_shape=(table, table, jax.ShapeDtypeStruct((INFO,), jnp.int32)),
        in_specs=[SMEM_SPEC] * 4,
        out_specs=(VMEM_SPEC, VMEM_SPEC, SMEM_SPEC),
        name="plan",
    )(occ_irrep, vir_irrep, pair_tiles, spin_mask)


def ring_kernel(
    steps,
    cap,
    inject_ref,
    info_ref,
    amp_ref,
    int_ref,
    a_ref,
    b_ref,
    own,
    land,
    leave,
    *rest,
):
    if cap == 2:
        amp_own, amp_out = rest[:2]
        rest = rest[2:]
        amp_in = rest[0]
        rest = rest[1:]
    own_in, own_send, own_recv, send, recv, kept, f_send, f_recv, a_send, a_recv = rest
    o = lax.axis_index("occ")
    v = lax.axis_index("vir")
    core = v % 2
    mate = v + 1 - 2 * core
    across = (v + 2) % 4
    pos = ring_pos(o)
    right = ring_place((pos + 1) % RING)
    left = ring_place((pos + RING - 1) % RING)
    half = SQUARE // 2

    def own_rows(k, side, group):
        rows = PER_SIDE * PIECE // GROUPS
        start = side * PER_SIDE * PIECE + group * rows
        to = own.at[pl.ds((2 * core + k) * half + start, rows)]

        def source(which):
            return int_ref.at[pl.ds(which * half + start, rows), pl.ds(k * SQUARE, SQUARE)]

        stay = pltpu.make_async_copy(source(core), to, own_in.at[k, side, group])
        give = pltpu.make_async_remote_copy(
            src_ref=source(1 - core),
            dst_ref=to,
            send_sem=own_send.at[k, side, group],
            recv_sem=own_recv.at[k, side, group],
            device_id=(o, mate),
            device_id_type=MESH,
        )
        return stay, give

    def own_parts(group):
        return [own_rows(k, side, group) for k in range(2) for side in range(2)]

    def amp_copy(k):
        return pltpu.make_async_copy(
            amp_ref.at[pl.ds(k // 2 * SQUARE, SQUARE), pl.ds(k % 2 * SQUARE, SQUARE)],
            amp_own.at[k],
            amp_in.at[k],
        )

    for group in range(GROUPS):
        for stay, _ in own_parts(group):
            stay.start()
    if cap == 2:
        for k in range(4):
            amp_copy(k).start()

    barrier = pltpu.get_barrier_semaphore()
    for target in ((right, v), (left, v), (o, mate), (o, across)):
        pl.semaphore_signal(barrier, inc=1, device_id=target, device_id_type=MESH)
    pl.semaphore_wait(barrier, 4)

    for group in range(GROUPS):
        for _, give in own_parts(group):
            give.start()

    def a_copy(which, index):
        slot = index // A_PARTS
        rows = SQUARE // A_PARTS
        cut = pl.ds(pl.multiple_of(index % A_PARTS * rows, rows), rows)
        owner = across if which == 2 else v
        if which == 2:
            source = a_ref.at[owner, slot, cut]
        elif cap == 2:
            source = amp_out.at[slot, cut]
        else:
            start = pl.multiple_of(slot // 2 * SQUARE + index % A_PARTS * rows, rows)
            source = amp_ref.at[pl.ds(start, rows), pl.ds(slot % 2 * SQUARE, SQUARE)]
        return pltpu.make_async_remote_copy(
            src_ref=source,
            dst_ref=a_ref.at[owner, slot, cut],
            send_sem=a_send.at[which, index],
            recv_sem=a_recv.at[which, index],
            device_id=(o, across if which == 0 else mate),
            device_id_type=MESH,
        )

    def hop(side, tau, p):
        return pltpu.make_async_remote_copy(
            src_ref=leave.at[side, p],
            dst_ref=land.at[side, tau],
            send_sem=send.at[side, p],
            recv_sem=recv.at[side, tau],
            device_id=(right if side == 0 else left, v),
            device_id_type=MESH,
        )

    def compose(side, turn, p, forward):
        tau = turn * CHUNK + p
        block = (inject_ref[side, pos, turn] >> (4 * p)) & 15
        pieces = [
            own[pl.ds((k * 2 * PER_SIDE + side * PER_SIDE + p) * PIECE, PIECE), :]
            for k in range(CHIP_BLOCKS)
        ]
        value = land[side, tau - LAG] if forward else pieces[0]
        for k in range(CHIP_BLOCKS):
            value = jnp.where(block == k + 1, pieces[k], value)
        leave[side, p] = value

    def pass_on(start, size, side):
        cut = pl.ds(start, size)
        stay = pltpu.make_async_copy(land.at[side, cut], b_ref.at[core, side, cut], kept)
        give = pltpu.make_async_remote_copy(
            src_ref=land.at[side, cut],
            dst_ref=b_ref.at[core, side, cut],
            send_sem=f_send,
            recv_sem=f_recv,
            device_id=(o, mate),
            device_id_type=MESH,
        )
        return stay, give

    def advance(turn, p, fresh):
        tau = turn * CHUNK + p
        for side in range(2):
            forward = not (fresh and p < LAG)
            if forward:
                hop(side, tau - LAG, (p - LAG) % CHUNK).wait_recv()
            if not fresh:
                hop(side, tau - SLOTS, p).wait_send()
            compose(side, turn, p, forward)
            hop(side, tau, p).start()

    def amp_start(slot):
        if cap == 2:
            pick = info_ref[SLOT_AT + slot]

            @pl.loop(0, SQUARE // 64)
            def _(part):
                cut = pl.ds(pl.multiple_of(part * 64, 64), 64)
                value = amp_own[0, cut]
                for k in range(1, 4):
                    value = jnp.where(pick == k, amp_own[k, cut], value)
                amp_out[slot, cut] = value

        for part in range(A_PARTS):
            for which in range(2):
                a_copy(which, slot * A_PARTS + part).start()

    def amp_forward(index):
        a_copy(0, index).wait_recv()
        a_copy(2, index).start()

    a_total = cap * A_PARTS
    full = steps // CHUNK
    spare = CHUNK // 2

    def hand_over(start, size):
        for side in range(2):
            for copy in pass_on(start, size, side):
                copy.start()

    def after(turn, p):
        if p == LAG - 1:
            hand_over(turn * CHUNK - spare, spare)
        if p == LAG - 1 + spare:
            hand_over(turn * CHUNK, spare)

    for p in range(CHUNK):
        if p % (PER_SIDE // GROUPS) == 0:
            for stay, give in own_parts(p // (PER_SIDE // GROUPS)):
                stay.wait()
                give.wait_recv()
        advance(0, p, True)
        if p == LAG - 1 and cap == 2:
            for k in range(4):
                amp_copy(k).wait()
        if p % 2 == 0 and LAG - 1 <= p < LAG - 1 + 2 * cap and p // 2 - 1 < min(cap, 2):
            amp_start(p // 2 - 1)
        if p == LAG - 1 + spare:
            hand_over(0, spare)
    for slot in range(2, cap):
        amp_start(slot)

    @pl.loop(1, full)
    def _(turn):
        @pl.when((turn >= A_LATE) & (turn < A_LATE + a_total))
        def _():
            amp_forward(turn - A_LATE)

        for p in range(CHUNK):
            advance(turn, p, False)
            after(turn, p)

    for p in range(steps % CHUNK):
        advance(full, p, False)
        after(full, p)

    for index in range(min(max(full - A_LATE, 0), a_total), a_total):
        amp_forward(index)
    for tau in range(steps - LAG, steps):
        for side in range(2):
            hop(side, tau, tau % CHUNK).wait_recv()
    hand_over(steps - spare, spare)
    for tau in range(steps - SLOTS, steps):
        for side in range(2):
            hop(side, tau, tau % CHUNK).wait_send()
    for group in range(GROUPS):
        for _, give in own_parts(group):
            give.wait_send()
    for which in range(3):
        for index in range(a_total):
            copy = a_copy(which, index)
            copy.wait_send()
            if which > 0:
                copy.wait_recv()
    every = pl.ds(0, steps)
    pltpu.make_async_copy(land, b_ref.at[core, :, every], kept).wait()
    total = pltpu.make_async_remote_copy(
        src_ref=land,
        dst_ref=b_ref.at[1 - core, :, every],
        send_sem=f_send,
        recv_sem=f_recv,
        device_id=(o, mate),
        device_id_type=MESH,
    )
    total.wait_send()
    total.wait_recv()


def ring(which, steps, cap, inject, info, amplitudes, integrals):
    square = (SQUARE, SQUARE)
    dma = pltpu.SemaphoreType.DMA
    kind = amplitudes.dtype
    amp_scratch = []
    if cap == 2:
        amp_scratch = [
            pltpu.VMEM((4,) + square, kind),
            pltpu.VMEM((2,) + square, kind),
            dma((4,)),
        ]
    return pl.pallas_call(
        functools.partial(ring_kernel, steps, cap),
        out_shape=(
            jax.ShapeDtypeStruct((4, 4) + square, kind),
            jax.ShapeDtypeStruct((2, 2, SPAN, PIECE, SQUARE), kind),
        ),
        in_specs=[SMEM_SPEC, SMEM_SPEC, ANY_SPEC, ANY_SPEC],
        out_specs=(ANY_SPEC, ANY_SPEC),
        scratch_shapes=[
            pltpu.VMEM((2 * SQUARE, SQUARE), kind),
            pltpu.VMEM((2, steps, PIECE, SQUARE), kind),
            pltpu.VMEM((2, SLOTS, PIECE, SQUARE), kind),
        ]
        + amp_scratch
        + [
            dma((2, 2, GROUPS)),
            dma((2, 2, GROUPS)),
            dma((2, 2, GROUPS)),
            dma((2, SLOTS)),
            dma((2, steps)),
            dma,
            dma,
            dma,
            dma((3, cap * A_PARTS)),
            dma((3, cap * A_PARTS)),
        ],
        compiler_params=pltpu.CompilerParams(
            collective_id=which, has_side_effects=True, vmem_limit_bytes=58 << 20
        ),
        name="ring",
    )(inject, info, amplitudes, integrals)


def ladder_kernel(
    info_ref,
    when_ref,
    occ_ref,
    vir_ref,
    amp_ref,
    int_ref,
    a_ref,
    b_ref,
    other_ref,
    out_ref,
    terms,
    a_buf,
    b_buf,
    other_buf,
    acc,
    result,
    blank,
    a_sem,
    b_sem,
    other_sem,
    out_sem,
    blank_sem,
):
    o = lax.axis_index("occ")
    v = lax.axis_index("vir")
    pos = ring_pos(o)
    wide = info_ref[WIDE_AT]
    rows = [info_ref[ROW_AT + 2 * o + r] for r in range(2)]

    def out_block(ref, b):
        return ref.at[
            pl.ds(pl.multiple_of(b // 2 * SQUARE, SQUARE), SQUARE),
            pl.ds(pl.multiple_of(b % 2 * SQUARE, SQUARE), SQUARE),
        ]

    def keep(b):
        return ((rows[b // 2] >> (2 * v + b % 2)) & 1) == 1

    count = jnp.int32(0)
    for b in range(4):
        alive = jnp.where(keep(b), 1, 0)
        for s in range(8):
            bit = alive * ((rows[b // 2] >> s) & 1)

            @pl.when(bit == 1)
            def _():
                terms[count] = b * 8 + s

            count = count + bit
    terms[count] = 64

    def fetch(j, slot):
        code = terms[j]
        b = code // 8
        s = code % 8
        r = b // 2
        tile = 2 * (v % 2) + b % 2
        src = s // 2
        block = r * 2 + s % 2

        @pl.when(src == v)
        def _():
            pltpu.make_async_copy(out_block(amp_ref, block), a_buf.at[slot], a_sem.at[slot]).start()

        @pl.when(src != v)
        def _():
            low = (rows[0] >> (2 * src)) & 3
            high = (rows[1] >> (2 * src)) & 3
            flags = low | (high << 2)
            below = flags & ((1 << block) - 1)
            rank = (below & 1) + ((below >> 1) & 1) + ((below >> 2) & 1)
            at = jnp.where(wide == 1, block, rank)
            pltpu.make_async_copy(a_ref.at[src, at], a_buf.at[slot], a_sem.at[slot]).start()

        @pl.when(s == o)
        def _():
            cols = pl.ds(pl.multiple_of(b % 2 * SQUARE, SQUARE), SQUARE)
            for k in range(2 * 2 * PER_SIDE):
                pltpu.make_async_copy(
                    int_ref.at[pl.ds(k * PIECE, PIECE), cols],
                    b_buf.at[slot, k // (2 * PER_SIDE), k // PER_SIDE % 2, k % PER_SIDE],
                    b_sem.at[slot],
                ).start()

        @pl.when(s != o)
        def _():
            flags = (info_ref[SENT_AT + s] >> (CHIP_BLOCKS * (v // 2))) & 15
            below = flags & ((1 << tile) - 1)
            rank = (below & 1) + ((below >> 1) & 1) + ((below >> 2) & 1)
            owner = ring_pos(s)
            for side in range(2):
                away = (pos - owner if side == 0 else owner - pos) % RING
                for p in range(PER_SIDE):
                    start = when_ref[side, owner, rank * PER_SIDE + p]
                    step = start + LAG * (away - 1)
                    pltpu.make_async_copy(
                        b_ref.at[:, side, step],
                        b_buf.at[slot, :, side, p],
                        b_sem.at[slot],
                    ).start()

    @pl.when(count > 0)
    def _():
        fetch(0, 0)

    def other_copy(b):
        return pltpu.make_async_copy(out_block(other_ref, b), other_buf.at[b], other_sem.at[b])

    def blank_copy(b):
        return pltpu.make_async_copy(blank, out_block(out_ref, b), blank_sem.at[b])

    for b in range(4):

        @pl.when(keep(b))
        def _():
            other_copy(b).start()

    blank[...] = jnp.zeros_like(blank)
    for b in range(4):

        @pl.when(jnp.logical_not(keep(b)))
        def _():
            blank_copy(b).start()

    def out_copy(b):
        return pltpu.make_async_copy(result.at[b % 2], out_block(out_ref, b), out_sem.at[b % 2])

    @pl.loop(0, count, init_carry=(jnp.int32(-1), jnp.int32(-1)))
    def last_out(j, carry):
        slot = j % 2

        @pl.when(j + 1 < count)
        def _():
            fetch(j + 1, 1 - slot)

        code = terms[j]
        b = code // 8
        before = jnp.where(j == 0, -1, terms[jnp.maximum(j - 1, 0)] // 8)
        fresh = before != b
        final = terms[j + 1] // 8 != b
        pltpu.make_async_copy(out_block(amp_ref, 0), a_buf.at[slot], a_sem.at[slot]).wait()
        pltpu.make_async_copy(b_buf.at[slot], b_buf.at[slot], b_sem.at[slot]).wait()

        def product(part):
            cols = pl.ds(pl.multiple_of(part * STEP_COLS, STEP_COLS), STEP_COLS)
            right = b_buf[slot, :, :, :, :, cols].reshape(SQUARE, STEP_COLS)
            return cols, jnp.dot(a_buf[slot], right, preferred_element_type=jnp.float32)

        @pl.when(jnp.logical_not(final) & fresh)
        def _():
            @pl.loop(0, SQUARE // STEP_COLS)
            def _(part):
                cols, term = product(part)
                acc[:, cols] = term

        @pl.when(jnp.logical_not(final) & jnp.logical_not(fresh))
        def _():
            @pl.loop(0, SQUARE // STEP_COLS)
            def _(part):
                cols, term = product(part)
                acc[:, cols] += term

        @pl.when(final)
        def _():
            @pl.when(fresh)
            def _():
                acc[...] = jnp.zeros_like(acc)

            other_copy(b).wait()
            pending = jnp.where(b % 2 == 0, carry[0], carry[1])

            @pl.when(pending >= 0)
            def _():
                out_copy(b).wait()

            @pl.loop(0, SQUARE // STEP_COLS)
            def _(part):
                cols, term = product(part)
                denom = occ_ref[b // 2] - vir_ref[b % 2, :, cols]
                total = (acc[:, cols] + term) + other_buf[b, :, cols].astype(jnp.float32)
                result[b % 2, :, cols] = (total / denom).astype(result.dtype)

            out_copy(b).start()

        even = jnp.where(final & (b % 2 == 0), b, carry[0])
        odd = jnp.where(final & (b % 2 == 1), b, carry[1])
        return even, odd

    for k in range(2):

        @pl.when(last_out[k] >= 0)
        def _():
            out_copy(k).wait()

    for b in range(4):

        @pl.when(jnp.logical_not(keep(b)))
        def _():
            blank_copy(b).wait()


def ladder(info, when, occ_sum, vir_sum, amplitudes, integrals, a_all, b_all, other_terms):
    square = (SQUARE, SQUARE)
    kind = amplitudes.dtype
    dma = pltpu.SemaphoreType.DMA
    return pl.pallas_call(
        ladder_kernel,
        out_shape=jax.ShapeDtypeStruct(other_terms.shape, other_terms.dtype),
        in_specs=[SMEM_SPEC, SMEM_SPEC, VMEM_SPEC, VMEM_SPEC] + [ANY_SPEC] * 5,
        out_specs=ANY_SPEC,
        scratch_shapes=[
            pltpu.SMEM((40,), jnp.int32),
            pltpu.VMEM((2,) + square, kind),
            pltpu.VMEM((2, 2, 2, PER_SIDE, PIECE, SQUARE), kind),
            pltpu.VMEM((4,) + square, kind),
            pltpu.VMEM(square, jnp.float32),
            pltpu.VMEM((2,) + square, kind),
            pltpu.VMEM(square, kind),
            dma((2,)),
            dma((2,)),
            dma((4,)),
            dma((2,)),
            dma((4,)),
        ],
        compiler_params=pltpu.CompilerParams(vmem_limit_bytes=48 << 20),
        name="ladder",
    )(info, when, occ_sum, vir_sum, amplitudes, integrals, a_all, b_all, other_terms)


def block_device(
    amplitudes,
    integrals,
    other_terms,
    occ_irrep,
    vir_irrep,
    pair_tiles,
    spin_mask,
    occ_energy,
    vir_energy,
):
    o = lax.axis_index("occ")
    v = lax.axis_index("vir")
    occ_tiles = occ_energy.reshape(OTILES, TILE)
    pair_occ = (occ_tiles[:, None, :, None] + occ_tiles[None, :, None, :]).reshape(-1, SQUARE)
    occ_sum = lax.dynamic_slice_in_dim(pair_occ, 2 * o, 2, 0)[:, :, None]
    vir_tiles = vir_energy.reshape(-1, TILE)
    tiles = lax.dynamic_slice_in_dim(pair_tiles, 2 * v, 2, 0)
    first = lookup(tiles[:, 0], vir_tiles)
    second = lookup(tiles[:, 1], vir_tiles)
    vir_sum = (first[:, :, None] + second[:, None, :]).reshape(2, 1, SQUARE)

    inject, when, info = plan(occ_irrep, vir_irrep, pair_tiles, spin_mask)
    inject, when, info, occ_sum, vir_sum = lax.optimization_barrier(
        (inject, when, info, occ_sum, vir_sum)
    )
    branches = [functools.partial(ring, k, steps, 2) for k, steps in enumerate(STEPS)]
    branches += [
        functools.partial(ring, WIDE_FROM + k, steps, 4) for k, steps in enumerate(WIDE_STEPS)
    ]
    a_all, b_all = lax.switch(
        info[VARIANT_AT], branches, inject, info, amplitudes, integrals
    )
    return ladder(info, when, occ_sum, vir_sum, amplitudes, integrals, a_all, b_all, other_terms)


def per_device(amplitudes, integrals, *rest):
    blocks = amplitudes.shape == (2 * SQUARE, 2 * SQUARE)
    blocks = blocks and integrals.shape == (SQUARE, 2 * SQUARE) and lax.axis_size("vir") == 4
    blocks = blocks and lax.axis_size("occ") == OTILES * OTILES // 2
    device = block_device if blocks else dense_device
    return device(amplitudes, integrals, *rest)


def solution(mesh):
    in_specs = (P("occ", "vir"), P("occ", "vir"), P("occ", "vir"), P(), P(), P(), P(), P(), P())
    out_specs = P("occ", "vir")
    return jax.shard_map(
        per_device, mesh=mesh, in_specs=in_specs, out_specs=out_specs, check_vma=False
    )
```

```python
import functools

import jax
import jax.numpy as jnp
from jax import lax
from jax.experimental import pallas as pl
from jax.experimental.pallas import tpu as pltpu
from jax.sharding import PartitionSpec as P

TILE = 32
OTILES = 4
SQUARE = TILE * TILE
STEP_COLS = 512


def lookup(index, table):
    hits = index[:, None] == jnp.arange(table.shape[0], dtype=jnp.int32)[None, :]
    return jnp.sum(
        jnp.where(hits[:, :, None], table[None, :, :], jnp.zeros_like(table)[None, :, :]), axis=1
    )


def symmetry(occ_irrep, vir_irrep, pair_tiles, spin_mask):
    first = lookup(pair_tiles[:, 0], vir_irrep[:, None])[:, 0]
    second = lookup(pair_tiles[:, 1], vir_irrep[:, None])[:, 0]
    pair_irrep = jnp.bitwise_xor(first, second)
    occ_pair = jnp.bitwise_xor(occ_irrep[:, None], occ_irrep[None, :]).reshape(-1)
    allowed = jnp.where(
        (occ_pair[:, None] == pair_irrep[None, :]) & (spin_mask == 1), 1.0, 0.0
    ).astype(jnp.float32)
    coupled = jnp.where(pair_irrep[:, None] == pair_irrep[None, :], 1.0, 0.0).astype(jnp.float32)
    return (allowed, coupled)


def dense_device(
    amplitudes,
    integrals,
    other_terms,
    occ_irrep,
    vir_irrep,
    pair_tiles,
    spin_mask,
    occ_energy,
    vir_energy,
):
    allowed, coupled = symmetry(occ_irrep, vir_irrep, pair_tiles, spin_mask)
    height = amplitudes.shape[0]
    width = amplitudes.shape[1]
    slab_height = integrals.shape[0]
    row_global = lax.axis_index("occ") * height + jnp.arange(height, dtype=jnp.int32)
    col_global = lax.axis_index("vir") * width + jnp.arange(width, dtype=jnp.int32)
    row_block = row_global // SQUARE
    col_pair = col_global // SQUARE
    row_allowed = lookup(row_block, allowed)
    amp_keep = lookup(col_pair, row_allowed.T).T
    masked_amp = jnp.where(amp_keep > 0.5, amplitudes, jnp.zeros_like(amplitudes))
    slab_pair = (
        lax.axis_index("occ") * slab_height + jnp.arange(slab_height, dtype=jnp.int32)
    ) // SQUARE
    int_keep = lookup(col_pair, lookup(slab_pair, coupled).T).T
    masked_slab = jnp.where(int_keep > 0.5, integrals, jnp.zeros_like(integrals))
    whole_amp = lax.all_gather(masked_amp, "vir", axis=1, tiled=True)
    whole_slab = lax.all_gather(masked_slab, "occ", axis=0, tiled=True)
    ladder = jnp.dot(whole_amp, whole_slab, preferred_element_type=jnp.float32)
    inner = row_global % SQUARE
    occ_first = row_block // OTILES * TILE + inner // TILE
    occ_second = row_block % OTILES * TILE + inner % TILE
    occ_sum = (
        lookup(occ_first, occ_energy[:, None])[:, 0] + lookup(occ_second, occ_energy[:, None])[:, 0]
    )
    col_inner = col_global % SQUARE
    tile_first = lookup(col_pair, pair_tiles[:, 0:1])[:, 0]
    tile_second = lookup(col_pair, pair_tiles[:, 1:2])[:, 0]
    vir_first = tile_first * TILE + col_inner // TILE
    vir_second = tile_second * TILE + col_inner % TILE
    vir_sum = (
        lookup(vir_first, vir_energy[:, None])[:, 0] + lookup(vir_second, vir_energy[:, None])[:, 0]
    )
    denom = occ_sum[:, None] - vir_sum[None, :]
    updated = amp_keep * ((ladder + other_terms.astype(jnp.float32)) / denom)
    return updated.astype(jnp.bfloat16)


RING = 8
CHIP_BLOCKS = 4
PIECE = 32
PER_SIDE = SQUARE // 4 // PIECE
SPAN = 256
LANES = 128
LAG = 3
BATCH = 4
SLOTS = 8
GROUPS = 4
A_PARTS = 4
A_LATE = 3
STEPS = (40, 52, 68, 76, 84, 88, 92, 100, 108, 116, 124, 140, 148, 176, 200, 248)
WIDE_FROM = len(STEPS)
WIDE_STEPS = (128, 176, 248)
MESH = pl.DeviceIdType.MESH
SMEM_SPEC = pl.BlockSpec(memory_space=pltpu.SMEM)
VMEM_SPEC = pl.BlockSpec(memory_space=pltpu.VMEM)
ANY_SPEC = pl.BlockSpec(memory_space=pl.ANY)
ROW_AT = 0
SENT_AT = 16
VARIANT_AT = 24
SLOT_AT = 25
WIDE_AT = 27
INFO = 32
SPIN_AT = 16
OCC_AT = 144
VIR_AT = 148


def ring_place(pos):
    late = pos // (RING // 2)
    return 2 * pos * (1 - late) + (2 * (RING - 1 - pos) + 1) * late


def ring_pos(o):
    odd = o % 2
    return (o // 2) * (1 - odd) + (RING - 1 - o // 2) * odd


def plan_kernel(small_ref, inject_ref, when_ref, info_ref):
    o = lax.axis_index("occ")
    v = lax.axis_index("vir")
    one = jnp.int32(1)

    def flag(condition):
        return jnp.where(condition, one, 0)

    pair = [
        small_ref[VIR_AT + small_ref[2 * t]] ^ small_ref[VIR_AT + small_ref[2 * t + 1]]
        for t in range(8)
    ]
    rows, spread = [], []
    for q in range(16):
        own = small_ref[OCC_AT + q // OTILES] ^ small_ref[OCC_AT + q % OTILES]
        row, wide_row = jnp.int32(0), jnp.int32(0)
        for t in range(8):
            hit = flag((own == pair[t]) & (small_ref[SPIN_AT + 8 * q + t] == 1))
            row = row | (hit << t)
            wide_row = wide_row | (hit << (4 * t))
        rows.append(row)
        spread.append(wide_row)
        info_ref[ROW_AT + q] = row
    far = [[], []]
    for s in range(8):
        at_pos = {}
        for chip in range(8):
            at_pos[ring_pos(chip)] = (spread[2 * chip] * ((rows[2 * chip] >> s) & 1)) | (
                spread[2 * chip + 1] * ((rows[2 * chip + 1] >> s) & 1)
            )
        for side in range(2):
            reach = jnp.int32(0)
            for away in range(1, RING):
                there = at_pos[(ring_pos(s) + (away if side == 0 else -away)) % RING]
                reach = (reach & ~(there * 15)) | (there * away)
            far[side].append(reach)
        sent = jnp.int32(0)
        for t in range(8):
            sent = sent | (flag(((far[0][s] >> (4 * t)) & 15) > 0) << t)
        info_ref[SENT_AT + s] = sent

    most = jnp.int32(0)
    for p in range(8):
        both = [rows[2 * p] , rows[2 * p + 1]]
        for w in range(4):
            bits = [(row >> (2 * w + k)) & 1 for row in both for k in range(2)]
            most = jnp.maximum(most, bits[0] + bits[1] + bits[2] + bits[3])
    mine = [info_ref[ROW_AT + 2 * o + r] for r in range(2)]
    rank = jnp.int32(0)
    picks = [jnp.int32(0), jnp.int32(0)]
    for k in range(4):
        bit = (mine[k // 2] >> (2 * v + k % 2)) & 1
        picks = [jnp.where((bit == 1) & (rank == j), k, picks[j]) for j in range(2)]
        rank = rank + bit
    for j in range(2):
        info_ref[SLOT_AT + j] = picks[j]
    wide = flag(most > 2)
    info_ref[WIDE_AT] = wide

    shape = (RING, LANES)
    at = lax.broadcasted_iota(jnp.int32, shape, 0)
    lane = lax.broadcasted_iota(jnp.int32, shape, 1)
    zero = jnp.minimum(at + lane, 0)
    totals, lists, travels = [], [], []
    bound = jnp.int32(0)
    for plane in range(2):
        total, listed = zero, zero
        travel = [zero, zero]
        whole = jnp.int32(0)
        for s in range(8):
            rank = jnp.int32(0)
            order = jnp.int32(0)
            hops = [jnp.int32(0), jnp.int32(0)]
            for k in range(CHIP_BLOCKS):
                reach = [(far[side][s] >> (4 * (CHIP_BLOCKS * plane + k))) & 15 for side in range(2)]
                bit = flag(reach[0] > 0)
                order = order | ((bit * k) << (2 * rank))
                hops = [hops[side] | (reach[side] << (4 * rank)) for side in range(2)]
                rank = rank + bit
            here = at == ring_pos(s)
            total = jnp.where(here, rank, total)
            listed = jnp.where(here, order, listed)
            travel = [jnp.where(here, hops[side], travel[side]) for side in range(2)]
            whole = whole + rank
        bound = jnp.maximum(bound, whole)
        totals.append(total)
        lists.append(listed)
        travels.append(travel)

    sims = [(plane, side) for plane in range(2) for side in range(2)]

    def big_step(turn, carry):
        out = []
        for (plane, side), (passing, counts, when, inject) in zip(sims, carry):
            counts = list(counts)
            word = zero
            for p in range(PER_SIDE):
                arrived = pltpu.roll(passing[0], 1 if side == 0 else RING - 1, 0)
                arrived = jnp.maximum(arrived - 1, 0)
                count = counts[p]
                starts = (arrived == 0) & (count < totals[plane])
                hops = (travels[plane][side] >> (4 * count)) & 15
                block = (lists[plane] >> (2 * count)) & 3
                passing = passing[1:] + (jnp.where(starts, hops, arrived),)
                now = turn * PER_SIDE + p
                when = jnp.where(starts & (lane == count * PER_SIDE + p), now, when)
                word = word | (jnp.where(starts, block + 1, 0) << (4 * p))
                counts[p] = jnp.where(starts, count + 1, count)
            inject = jnp.where(lane == turn, word, inject)
            out.append((passing, tuple(counts), when, inject))
        return tuple(out)

    first = tuple(((zero,) * LAG, (zero,) * PER_SIDE, zero, zero) for _ in sims)
    done = lax.fori_loop(0, bound, big_step, first)
    last = zero
    chip_plane = v // 2
    for side in range(2):
        when_ref[side] = jnp.where(chip_plane == 0, done[side][2], done[2 + side][2])
        inject_ref[side] = jnp.where(chip_plane == 0, done[side][3], done[2 + side][3])
    rank = jnp.minimum(lane // PER_SIDE, CHIP_BLOCKS)
    for (plane, side), state in zip(sims, done):
        hops = (travels[plane][side] >> (4 * rank)) & 15
        last = jnp.maximum(last, jnp.where(rank < totals[plane], state[2] + LAG * (hops - 1), 0))
    need = jnp.max(last) + 1
    variant = jnp.int32(0)
    for steps in STEPS[:-1]:
        variant = variant + flag(need > steps)
    wide_variant = jnp.int32(WIDE_FROM)
    for steps in WIDE_STEPS[:-1]:
        wide_variant = wide_variant + flag(need > steps)
    info_ref[VARIANT_AT] = jnp.where(wide == 1, wide_variant, variant)


def plan(occ_irrep, vir_irrep, pair_tiles, spin_mask):
    small = jnp.concatenate(
        [pair_tiles.reshape(-1), spin_mask.reshape(-1), occ_irrep, vir_irrep]
    )
    table = jax.ShapeDtypeStruct((2, RING, LANES), jnp.int32)
    return pl.pallas_call(
        plan_kernel,
        out_shape=(table, table, jax.ShapeDtypeStruct((INFO,), jnp.int32)),
        in_specs=[SMEM_SPEC],
        out_specs=(VMEM_SPEC, VMEM_SPEC, SMEM_SPEC),
        name="plan",
    )(small)


def ring_kernel(
    steps,
    cap,
    inject_ref,
    info_ref,
    amp_ref,
    int_ref,
    a_ref,
    b_ref,
    own,
    land,
    leave,
    *rest,
):
    if cap == 2:
        amp_own, amp_out = rest[:2]
        rest = rest[2:]
        amp_in = rest[0]
        rest = rest[1:]
    own_in, own_send, own_recv, send, recv, kept, f_send, f_recv, a_send, a_recv = rest
    o = lax.axis_index("occ")
    v = lax.axis_index("vir")
    core = v % 2
    mate = v + 1 - 2 * core
    across = (v + 2) % 4
    pos = ring_pos(o)
    right = ring_place((pos + 1) % RING)
    left = ring_place((pos + RING - 1) % RING)
    half = SQUARE // 2
    a_total = cap * A_PARTS

    def own_rows(k, side, group):
        rows = PER_SIDE * PIECE // GROUPS
        start = side * PER_SIDE * PIECE + group * rows
        to = own.at[pl.ds(pl.multiple_of((2 * core + k) * half + start, rows), rows)]

        def source(which):
            row = pl.multiple_of(which * half + start, rows)
            return int_ref.at[pl.ds(row, rows), pl.ds(k * SQUARE, SQUARE)]

        stay = pltpu.make_async_copy(source(core), to, own_in.at[k, side, group])
        give = pltpu.make_async_remote_copy(
            src_ref=source(1 - core),
            dst_ref=to,
            send_sem=own_send.at[k, side, group],
            recv_sem=own_recv.at[k, side, group],
            device_id=(o, mate),
            device_id_type=MESH,
        )
        return stay, give

    def own_parts(group):
        return [own_rows(k, side, group) for k in range(2) for side in range(2)]

    def amp_copy(k):
        return pltpu.make_async_copy(
            amp_ref.at[pl.ds(k // 2 * SQUARE, SQUARE), pl.ds(k % 2 * SQUARE, SQUARE)],
            amp_own.at[k],
            amp_in.at[k],
        )

    for group in range(GROUPS):
        for stay, _ in own_parts(group):
            stay.start()
    if cap == 2:
        for k in range(4):
            amp_copy(k).start()

    barrier = pltpu.get_barrier_semaphore()
    for target in ((right, v), (left, v), (o, mate), (o, across)):
        pl.semaphore_signal(barrier, inc=1, device_id=target, device_id_type=MESH)
    pl.semaphore_wait(barrier, 4)

    for group in range(GROUPS):
        for _, give in own_parts(group):
            give.start()

    def a_copy(which, index):
        slot = index // A_PARTS
        rows = SQUARE // A_PARTS
        cut = pl.ds(pl.multiple_of(index % A_PARTS * rows, rows), rows)
        owner = across if which == 2 else v
        if which == 2:
            source = a_ref.at[owner, slot, cut]
        elif cap == 2:
            source = amp_out.at[slot, cut]
        else:
            start = pl.multiple_of(slot // 2 * SQUARE + index % A_PARTS * rows, rows)
            source = amp_ref.at[
                pl.ds(start, rows), pl.ds(pl.multiple_of(slot % 2 * SQUARE, SQUARE), SQUARE)
            ]
        return pltpu.make_async_remote_copy(
            src_ref=source,
            dst_ref=a_ref.at[owner, slot, cut],
            send_sem=a_send.at[which, index],
            recv_sem=a_recv.at[which, index],
            device_id=(o, across if which == 0 else mate),
            device_id_type=MESH,
        )

    def hop(side, tau):
        return pltpu.make_async_remote_copy(
            src_ref=leave.at[side, tau % SLOTS],
            dst_ref=land.at[side, tau],
            send_sem=send.at[side, tau % SLOTS],
            recv_sem=recv.at[side, tau],
            device_id=(right if side == 0 else left, v),
            device_id_type=MESH,
        )

    def compose(side, tau, forward):
        p = tau % PER_SIDE
        block = (inject_ref[side, pos, tau // PER_SIDE] >> (4 * p)) & 15
        pieces = []
        for k in range(CHIP_BLOCKS):
            row = ((2 * k + side) * PER_SIDE + p) * PIECE
            pieces.append(own[pl.ds(pl.multiple_of(row, PIECE), PIECE), :])
        value = land[side, tau - LAG] if forward else pieces[0]
        for k in range(CHIP_BLOCKS):
            value = jnp.where(block == k + 1, pieces[k], value)
        leave[side, tau % SLOTS] = value

    def pass_on(start, size, side):
        cut = pl.ds(start, size)
        stay = pltpu.make_async_copy(land.at[side, cut], b_ref.at[core, side, cut], kept)
        give = pltpu.make_async_remote_copy(
            src_ref=land.at[side, cut],
            dst_ref=b_ref.at[core, side, cut],
            send_sem=f_send,
            recv_sem=f_recv,
            device_id=(o, mate),
            device_id_type=MESH,
        )
        return stay, give

    def amp_start(slot):
        if cap == 2:
            pick = jnp.where(slot == 0, info_ref[SLOT_AT], info_ref[SLOT_AT + 1])

            @pl.loop(0, SQUARE // 64)
            def _(part):
                cut = pl.ds(pl.multiple_of(part * 64, 64), 64)
                value = amp_own[0, cut]
                for k in range(1, 4):
                    value = jnp.where(pick == k, amp_own[k, cut], value)
                amp_out[slot, cut] = value

        for part in range(A_PARTS):
            for which in range(2):
                a_copy(which, slot * A_PARTS + part).start()

    def amp_forward(index):
        a_copy(0, index).wait_recv()
        a_copy(2, index).start()

    def hand_over(start):
        for side in range(2):
            for copy in pass_on(start, BATCH, side):
                copy.start()

    def own_wait(tau):
        @pl.when((tau < PER_SIDE) & (tau % (PER_SIDE // GROUPS) == 0))
        def _():
            for stay, give in own_parts(tau // (PER_SIDE // GROUPS)):
                stay.wait()
                give.wait_recv()

    @pl.loop(0, LAG)
    def _(tau):
        own_wait(tau)
        for side in range(2):
            compose(side, tau, False)
            hop(side, tau).start()

    if cap == 2:
        for k in range(4):
            amp_copy(k).wait()

    @pl.loop(LAG, steps)
    def _(tau):
        own_wait(tau)
        for side in range(2):
            hop(side, tau - LAG).wait_recv()

            @pl.when(tau >= SLOTS)
            def _():
                hop(side, tau - SLOTS).wait_send()

            compose(side, tau, True)
            hop(side, tau).start()

        @pl.when((tau >= BATCH + LAG - 1) & (tau % BATCH == (LAG - 1) % BATCH))
        def _():
            hand_over(tau - (BATCH + LAG - 1))

        @pl.when((tau % 2 == LAG % 2) & (tau < LAG + 2 * cap))
        def _():
            amp_start((tau - LAG) // 2)

        late = tau // PER_SIDE - A_LATE

        @pl.when((tau % PER_SIDE == 0) & (late >= 0) & (late < a_total))
        def _():
            amp_forward(late)

    done = min(max((steps - 1) // PER_SIDE - A_LATE + 1, 0), a_total)

    @pl.loop(done, a_total)
    def _(index):
        amp_forward(index)

    @pl.loop(steps - LAG, steps)
    def _(tau):
        for side in range(2):
            hop(side, tau).wait_recv()

    hand_over(steps - BATCH)

    @pl.loop(steps - SLOTS, steps)
    def _(tau):
        for side in range(2):
            hop(side, tau).wait_send()

    @pl.loop(0, GROUPS)
    def _(group):
        for _, give in own_parts(group):
            give.wait_send()

    @pl.loop(0, a_total)
    def _(index):
        for which in range(3):
            copy = a_copy(which, index)
            copy.wait_send()
            if which > 0:
                copy.wait_recv()

    every = pl.ds(0, steps)
    pltpu.make_async_copy(land, b_ref.at[core, :, every], kept).wait()
    total = pltpu.make_async_remote_copy(
        src_ref=land,
        dst_ref=b_ref.at[1 - core, :, every],
        send_sem=f_send,
        recv_sem=f_recv,
        device_id=(o, mate),
        device_id_type=MESH,
    )
    total.wait_send()
    total.wait_recv()


def ring(which, steps, cap, inject, info, amplitudes, integrals):
    square = (SQUARE, SQUARE)
    dma = pltpu.SemaphoreType.DMA
    kind = amplitudes.dtype
    amp_scratch = []
    if cap == 2:
        amp_scratch = [
            pltpu.VMEM((4,) + square, kind),
            pltpu.VMEM((2,) + square, kind),
            dma((4,)),
        ]
    return pl.pallas_call(
        functools.partial(ring_kernel, steps, cap),
        out_shape=(
            jax.ShapeDtypeStruct((4, 4) + square, kind),
            jax.ShapeDtypeStruct((2, 2, SPAN, PIECE, SQUARE), kind),
        ),
        in_specs=[SMEM_SPEC, SMEM_SPEC, ANY_SPEC, ANY_SPEC],
        out_specs=(ANY_SPEC, ANY_SPEC),
        scratch_shapes=[
            pltpu.VMEM((2 * SQUARE, SQUARE), kind),
            pltpu.VMEM((2, steps, PIECE, SQUARE), kind),
            pltpu.VMEM((2, SLOTS, PIECE, SQUARE), kind),
        ]
        + amp_scratch
        + [
            dma((2, 2, GROUPS)),
            dma((2, 2, GROUPS)),
            dma((2, 2, GROUPS)),
            dma((2, SLOTS)),
            dma((2, steps)),
            dma,
            dma,
            dma,
            dma((3, cap * A_PARTS)),
            dma((3, cap * A_PARTS)),
        ],
        compiler_params=pltpu.CompilerParams(
            collective_id=which, has_side_effects=True, vmem_limit_bytes=58 << 20
        ),
        name="ring",
    )(inject, info, amplitudes, integrals)


def ladder_kernel(
    info_ref,
    when_ref,
    occ_ref,
    vir_ref,
    amp_ref,
    int_ref,
    a_ref,
    b_ref,
    other_ref,
    out_ref,
    terms,
    a_buf,
    b_buf,
    other_buf,
    acc,
    result,
    blank,
    a_sem,
    b_sem,
    other_sem,
    out_sem,
    blank_sem,
):
    o = lax.axis_index("occ")
    v = lax.axis_index("vir")
    pos = ring_pos(o)
    wide = info_ref[WIDE_AT]
    rows = [info_ref[ROW_AT + 2 * o + r] for r in range(2)]

    def out_block(ref, b):
        return ref.at[
            pl.ds(pl.multiple_of(b // 2 * SQUARE, SQUARE), SQUARE),
            pl.ds(pl.multiple_of(b % 2 * SQUARE, SQUARE), SQUARE),
        ]

    def keep(b):
        return ((rows[b // 2] >> (2 * v + b % 2)) & 1) == 1

    count = jnp.int32(0)
    for b in range(4):
        alive = jnp.where(keep(b), 1, 0)
        for s in range(8):
            bit = alive * ((rows[b // 2] >> s) & 1)

            @pl.when(bit == 1)
            def _():
                terms[count] = b * 8 + s

            count = count + bit
    terms[count] = 64

    def fetch(j, slot):
        code = terms[j]
        b = code // 8
        s = code % 8
        r = b // 2
        tile = 2 * (v % 2) + b % 2
        src = s // 2
        block = r * 2 + s % 2

        @pl.when(src == v)
        def _():
            pltpu.make_async_copy(out_block(amp_ref, block), a_buf.at[slot], a_sem.at[slot]).start()

        @pl.when(src != v)
        def _():
            low = (rows[0] >> (2 * src)) & 3
            high = (rows[1] >> (2 * src)) & 3
            flags = low | (high << 2)
            below = flags & ((1 << block) - 1)
            rank = (below & 1) + ((below >> 1) & 1) + ((below >> 2) & 1)
            at = jnp.where(wide == 1, block, rank)
            pltpu.make_async_copy(a_ref.at[src, at], a_buf.at[slot], a_sem.at[slot]).start()

        @pl.when(s == o)
        def _():
            cols = pl.ds(pl.multiple_of(b % 2 * SQUARE, SQUARE), SQUARE)
            for k in range(2 * 2 * PER_SIDE):
                pltpu.make_async_copy(
                    int_ref.at[pl.ds(k * PIECE, PIECE), cols],
                    b_buf.at[slot, k // (2 * PER_SIDE), k // PER_SIDE % 2, k % PER_SIDE],
                    b_sem.at[slot],
                ).start()

        @pl.when(s != o)
        def _():
            flags = (info_ref[SENT_AT + s] >> (CHIP_BLOCKS * (v // 2))) & 15
            below = flags & ((1 << tile) - 1)
            rank = (below & 1) + ((below >> 1) & 1) + ((below >> 2) & 1)
            owner = ring_pos(s)
            for side in range(2):
                away = (pos - owner if side == 0 else owner - pos) % RING
                for p in range(PER_SIDE):
                    start = when_ref[side, owner, rank * PER_SIDE + p]
                    step = start + LAG * (away - 1)
                    pltpu.make_async_copy(
                        b_ref.at[:, side, step],
                        b_buf.at[slot, :, side, p],
                        b_sem.at[slot],
                    ).start()

    @pl.when(count > 0)
    def _():
        fetch(0, 0)

    def other_copy(b):
        return pltpu.make_async_copy(out_block(other_ref, b), other_buf.at[b], other_sem.at[b])

    def blank_copy(b):
        return pltpu.make_async_copy(blank, out_block(out_ref, b), blank_sem.at[b])

    for b in range(4):

        @pl.when(keep(b))
        def _():
            other_copy(b).start()

    blank[...] = jnp.zeros_like(blank)
    for b in range(4):

        @pl.when(jnp.logical_not(keep(b)))
        def _():
            blank_copy(b).start()

    def out_copy(b):
        return pltpu.make_async_copy(result.at[b % 2], out_block(out_ref, b), out_sem.at[b % 2])

    @pl.loop(0, count, init_carry=(jnp.int32(-1), jnp.int32(-1)))
    def last_out(j, carry):
        slot = j % 2

        @pl.when(j + 1 < count)
        def _():
            fetch(j + 1, 1 - slot)

        code = terms[j]
        b = code // 8
        before = jnp.where(j == 0, -1, terms[jnp.maximum(j - 1, 0)] // 8)
        fresh = before != b
        final = terms[j + 1] // 8 != b
        pltpu.make_async_copy(out_block(amp_ref, 0), a_buf.at[slot], a_sem.at[slot]).wait()
        pltpu.make_async_copy(b_buf.at[slot], b_buf.at[slot], b_sem.at[slot]).wait()

        def product(part):
            cols = pl.ds(pl.multiple_of(part * STEP_COLS, STEP_COLS), STEP_COLS)
            right = b_buf[slot, :, :, :, :, cols].reshape(SQUARE, STEP_COLS)
            return cols, jnp.dot(a_buf[slot], right, preferred_element_type=jnp.float32)

        @pl.when(fresh)
        def _():
            acc[...] = jnp.zeros_like(acc)

        @pl.when(jnp.logical_not(final))
        def _():
            @pl.loop(0, SQUARE // STEP_COLS)
            def _(part):
                cols, term = product(part)
                acc[:, cols] += term

        @pl.when(final)
        def _():
            other_copy(b).wait()
            pending = jnp.where(b % 2 == 0, carry[0], carry[1])

            @pl.when(pending >= 0)
            def _():
                out_copy(b).wait()

            @pl.loop(0, SQUARE // STEP_COLS)
            def _(part):
                cols, term = product(part)
                denom = occ_ref[b // 2] - vir_ref[b % 2, :, cols]
                total = (acc[:, cols] + term) + other_buf[b, :, cols].astype(jnp.float32)
                result[b % 2, :, cols] = (total / denom).astype(result.dtype)

            out_copy(b).start()

        even = jnp.where(final & (b % 2 == 0), b, carry[0])
        odd = jnp.where(final & (b % 2 == 1), b, carry[1])
        return even, odd

    for k in range(2):

        @pl.when(last_out[k] >= 0)
        def _():
            out_copy(k).wait()

    for b in range(4):

        @pl.when(jnp.logical_not(keep(b)))
        def _():
            blank_copy(b).wait()


def ladder(info, when, occ_sum, vir_sum, amplitudes, integrals, a_all, b_all, other_terms):
    square = (SQUARE, SQUARE)
    kind = amplitudes.dtype
    dma = pltpu.SemaphoreType.DMA
    return pl.pallas_call(
        ladder_kernel,
        out_shape=jax.ShapeDtypeStruct(other_terms.shape, other_terms.dtype),
        in_specs=[SMEM_SPEC, SMEM_SPEC, VMEM_SPEC, VMEM_SPEC] + [ANY_SPEC] * 5,
        out_specs=ANY_SPEC,
        scratch_shapes=[
            pltpu.SMEM((40,), jnp.int32),
            pltpu.VMEM((2,) + square, kind),
            pltpu.VMEM((2, 2, 2, PER_SIDE, PIECE, SQUARE), kind),
            pltpu.VMEM((4,) + square, kind),
            pltpu.VMEM(square, jnp.float32),
            pltpu.VMEM((2,) + square, kind),
            pltpu.VMEM(square, kind),
            dma((2,)),
            dma((2,)),
            dma((4,)),
            dma((2,)),
            dma((4,)),
        ],
        compiler_params=pltpu.CompilerParams(vmem_limit_bytes=48 << 20),
        name="ladder",
    )(info, when, occ_sum, vir_sum, amplitudes, integrals, a_all, b_all, other_terms)


def block_device(
    amplitudes,
    integrals,
    other_terms,
    occ_irrep,
    vir_irrep,
    pair_tiles,
    spin_mask,
    occ_energy,
    vir_energy,
):
    o = lax.axis_index("occ")
    v = lax.axis_index("vir")
    occ_tiles = occ_energy.reshape(OTILES, TILE)
    pair_occ = (occ_tiles[:, None, :, None] + occ_tiles[None, :, None, :]).reshape(-1, SQUARE)
    occ_sum = lax.dynamic_slice_in_dim(pair_occ, 2 * o, 2, 0)[:, :, None]
    vir_tiles = vir_energy.reshape(-1, TILE)
    tiles = lax.dynamic_slice_in_dim(pair_tiles, 2 * v, 2, 0)
    first = lookup(tiles[:, 0], vir_tiles)
    second = lookup(tiles[:, 1], vir_tiles)
    vir_sum = (first[:, :, None] + second[:, None, :]).reshape(2, 1, SQUARE)

    inject, when, info = plan(occ_irrep, vir_irrep, pair_tiles, spin_mask)
    inject, when, info, occ_sum, vir_sum = lax.optimization_barrier(
        (inject, when, info, occ_sum, vir_sum)
    )
    branches = [functools.partial(ring, k, steps, 2) for k, steps in enumerate(STEPS)]
    branches += [
        functools.partial(ring, WIDE_FROM + k, steps, 4) for k, steps in enumerate(WIDE_STEPS)
    ]
    a_all, b_all = lax.switch(
        info[VARIANT_AT], branches, inject, info, amplitudes, integrals
    )
    return ladder(info, when, occ_sum, vir_sum, amplitudes, integrals, a_all, b_all, other_terms)


def per_device(amplitudes, integrals, *rest):
    blocks = amplitudes.shape == (2 * SQUARE, 2 * SQUARE)
    blocks = blocks and integrals.shape == (SQUARE, 2 * SQUARE) and lax.axis_size("vir") == 4
    blocks = blocks and lax.axis_size("occ") == OTILES * OTILES // 2
    device = block_device if blocks else dense_device
    return device(amplitudes, integrals, *rest)


def solution(mesh):
    in_specs = (P("occ", "vir"), P("occ", "vir"), P("occ", "vir"), P(), P(), P(), P(), P(), P())
    out_specs = P("occ", "vir")
    return jax.shard_map(
        per_device, mesh=mesh, in_specs=in_specs, out_specs=out_specs, check_vma=False
    )
```

```python
import functools

import jax
import jax.numpy as jnp
from jax import lax
from jax.experimental import pallas as pl
from jax.experimental.pallas import tpu as pltpu
from jax.sharding import PartitionSpec as P

TILE = 32
OTILES = 4
SQUARE = TILE * TILE
STEP_COLS = 512


def lookup(index, table):
    hits = index[:, None] == jnp.arange(table.shape[0], dtype=jnp.int32)[None, :]
    return jnp.sum(
        jnp.where(hits[:, :, None], table[None, :, :], jnp.zeros_like(table)[None, :, :]), axis=1
    )


def symmetry(occ_irrep, vir_irrep, pair_tiles, spin_mask):
    first = lookup(pair_tiles[:, 0], vir_irrep[:, None])[:, 0]
    second = lookup(pair_tiles[:, 1], vir_irrep[:, None])[:, 0]
    pair_irrep = jnp.bitwise_xor(first, second)
    occ_pair = jnp.bitwise_xor(occ_irrep[:, None], occ_irrep[None, :]).reshape(-1)
    allowed = jnp.where(
        (occ_pair[:, None] == pair_irrep[None, :]) & (spin_mask == 1), 1.0, 0.0
    ).astype(jnp.float32)
    coupled = jnp.where(pair_irrep[:, None] == pair_irrep[None, :], 1.0, 0.0).astype(jnp.float32)
    return (allowed, coupled)


def dense_device(
    amplitudes,
    integrals,
    other_terms,
    occ_irrep,
    vir_irrep,
    pair_tiles,
    spin_mask,
    occ_energy,
    vir_energy,
):
    allowed, coupled = symmetry(occ_irrep, vir_irrep, pair_tiles, spin_mask)
    height = amplitudes.shape[0]
    width = amplitudes.shape[1]
    slab_height = integrals.shape[0]
    row_global = lax.axis_index("occ") * height + jnp.arange(height, dtype=jnp.int32)
    col_global = lax.axis_index("vir") * width + jnp.arange(width, dtype=jnp.int32)
    row_block = row_global // SQUARE
    col_pair = col_global // SQUARE
    row_allowed = lookup(row_block, allowed)
    amp_keep = lookup(col_pair, row_allowed.T).T
    masked_amp = jnp.where(amp_keep > 0.5, amplitudes, jnp.zeros_like(amplitudes))
    slab_pair = (
        lax.axis_index("occ") * slab_height + jnp.arange(slab_height, dtype=jnp.int32)
    ) // SQUARE
    int_keep = lookup(col_pair, lookup(slab_pair, coupled).T).T
    masked_slab = jnp.where(int_keep > 0.5, integrals, jnp.zeros_like(integrals))
    whole_amp = lax.all_gather(masked_amp, "vir", axis=1, tiled=True)
    whole_slab = lax.all_gather(masked_slab, "occ", axis=0, tiled=True)
    ladder = jnp.dot(whole_amp, whole_slab, preferred_element_type=jnp.float32)
    inner = row_global % SQUARE
    occ_first = row_block // OTILES * TILE + inner // TILE
    occ_second = row_block % OTILES * TILE + inner % TILE
    occ_sum = (
        lookup(occ_first, occ_energy[:, None])[:, 0] + lookup(occ_second, occ_energy[:, None])[:, 0]
    )
    col_inner = col_global % SQUARE
    tile_first = lookup(col_pair, pair_tiles[:, 0:1])[:, 0]
    tile_second = lookup(col_pair, pair_tiles[:, 1:2])[:, 0]
    vir_first = tile_first * TILE + col_inner // TILE
    vir_second = tile_second * TILE + col_inner % TILE
    vir_sum = (
        lookup(vir_first, vir_energy[:, None])[:, 0] + lookup(vir_second, vir_energy[:, None])[:, 0]
    )
    denom = occ_sum[:, None] - vir_sum[None, :]
    updated = amp_keep * ((ladder + other_terms.astype(jnp.float32)) / denom)
    return updated.astype(jnp.bfloat16)


RING = 8
CHIP_BLOCKS = 4
PIECE = 32
PER_SIDE = SQUARE // 4 // PIECE
SPAN = 256
LANES = 128
LAG = 3
BATCH = 4
SLOTS = 8
GROUPS = 4
A_PARTS = 4
A_LATE = 3
STEPS = (40, 52, 68, 76, 84, 88, 92, 100, 108, 116, 124, 140, 156, 180, 248)
WIDE_FROM = len(STEPS)
WIDE_STEPS = (128, 148, 180, 248)
MESH = pl.DeviceIdType.MESH
SMEM_SPEC = pl.BlockSpec(memory_space=pltpu.SMEM)
VMEM_SPEC = pl.BlockSpec(memory_space=pltpu.VMEM)
ANY_SPEC = pl.BlockSpec(memory_space=pl.ANY)
ROW_AT = 0
SENT_AT = 16
VARIANT_AT = 24
SLOT_AT = 25
WIDE_AT = 27
INFO = 32
SPIN_AT = 16
OCC_AT = 144
VIR_AT = 148


def ring_place(pos):
    late = pos // (RING // 2)
    return 2 * pos * (1 - late) + (2 * (RING - 1 - pos) + 1) * late


def ring_pos(o):
    odd = o % 2
    return (o // 2) * (1 - odd) + (RING - 1 - o // 2) * odd


def plan_kernel(small_ref, inject_ref, when_ref, info_ref):
    o = lax.axis_index("occ")
    v = lax.axis_index("vir")
    one = jnp.int32(1)

    def flag(condition):
        return jnp.where(condition, one, 0)

    pair = [
        small_ref[VIR_AT + small_ref[2 * t]] ^ small_ref[VIR_AT + small_ref[2 * t + 1]]
        for t in range(8)
    ]
    rows, spread = [], []
    for q in range(16):
        own = small_ref[OCC_AT + q // OTILES] ^ small_ref[OCC_AT + q % OTILES]
        row, wide_row = jnp.int32(0), jnp.int32(0)
        for t in range(8):
            hit = flag((own == pair[t]) & (small_ref[SPIN_AT + 8 * q + t] == 1))
            row = row | (hit << t)
            wide_row = wide_row | (hit << (4 * t))
        rows.append(row)
        spread.append(wide_row)
        info_ref[ROW_AT + q] = row
    far = [[], []]
    for s in range(8):
        at_pos = {}
        for chip in range(8):
            at_pos[ring_pos(chip)] = (spread[2 * chip] * ((rows[2 * chip] >> s) & 1)) | (
                spread[2 * chip + 1] * ((rows[2 * chip + 1] >> s) & 1)
            )
        for side in range(2):
            reach = jnp.int32(0)
            for away in range(1, RING):
                there = at_pos[(ring_pos(s) + (away if side == 0 else -away)) % RING]
                reach = (reach & ~(there * 15)) | (there * away)
            far[side].append(reach)
        sent = jnp.int32(0)
        for t in range(8):
            sent = sent | (flag(((far[0][s] >> (4 * t)) & 15) > 0) << t)
        info_ref[SENT_AT + s] = sent

    most = jnp.int32(0)
    for p in range(8):
        both = [rows[2 * p] , rows[2 * p + 1]]
        for w in range(4):
            bits = [(row >> (2 * w + k)) & 1 for row in both for k in range(2)]
            most = jnp.maximum(most, bits[0] + bits[1] + bits[2] + bits[3])
    mine = [info_ref[ROW_AT + 2 * o + r] for r in range(2)]
    rank = jnp.int32(0)
    picks = [jnp.int32(0), jnp.int32(0)]
    for k in range(4):
        bit = (mine[k // 2] >> (2 * v + k % 2)) & 1
        picks = [jnp.where((bit == 1) & (rank == j), k, picks[j]) for j in range(2)]
        rank = rank + bit
    for j in range(2):
        info_ref[SLOT_AT + j] = picks[j]
    wide = flag(most > 2)
    info_ref[WIDE_AT] = wide

    shape = (RING, LANES)
    at = lax.broadcasted_iota(jnp.int32, shape, 0)
    lane = lax.broadcasted_iota(jnp.int32, shape, 1)
    zero = jnp.minimum(at + lane, 0)
    totals, lists, travels = [], [], []
    bound = jnp.int32(0)
    for plane in range(2):
        total, listed = zero, zero
        travel = [zero, zero]
        whole = jnp.int32(0)
        for s in range(8):
            rank = jnp.int32(0)
            order = jnp.int32(0)
            hops = [jnp.int32(0), jnp.int32(0)]
            for k in range(CHIP_BLOCKS):
                reach = [(far[side][s] >> (4 * (CHIP_BLOCKS * plane + k))) & 15 for side in range(2)]
                bit = flag(reach[0] > 0)
                order = order | ((bit * k) << (2 * rank))
                hops = [hops[side] | (reach[side] << (4 * rank)) for side in range(2)]
                rank = rank + bit
            here = at == ring_pos(s)
            total = jnp.where(here, rank, total)
            listed = jnp.where(here, order, listed)
            travel = [jnp.where(here, hops[side], travel[side]) for side in range(2)]
            whole = whole + rank
        bound = jnp.maximum(bound, whole)
        totals.append(total)
        lists.append(listed)
        travels.append(travel)

    sims = [(plane, side) for plane in range(2) for side in range(2)]

    def big_step(turn, carry):
        out = []
        for (plane, side), (passing, counts, when, inject) in zip(sims, carry):
            counts = list(counts)
            word = zero
            for p in range(PER_SIDE):
                arrived = pltpu.roll(passing[0], 1 if side == 0 else RING - 1, 0)
                arrived = jnp.maximum(arrived - 1, 0)
                count = counts[p]
                starts = (arrived == 0) & (count < totals[plane])
                hops = (travels[plane][side] >> (4 * count)) & 15
                block = (lists[plane] >> (2 * count)) & 3
                passing = passing[1:] + (jnp.where(starts, hops, arrived),)
                now = turn * PER_SIDE + p
                when = jnp.where(starts & (lane == count * PER_SIDE + p), now, when)
                word = word | (jnp.where(starts, block + 1, 0) << (4 * p))
                counts[p] = jnp.where(starts, count + 1, count)
            inject = jnp.where(lane == turn, word, inject)
            out.append((passing, tuple(counts), when, inject))
        return tuple(out)

    first = tuple(((zero,) * LAG, (zero,) * PER_SIDE, zero, zero) for _ in sims)
    done = lax.fori_loop(0, bound, big_step, first)
    last = zero
    chip_plane = v // 2
    for side in range(2):
        when_ref[side] = jnp.where(chip_plane == 0, done[side][2], done[2 + side][2])
        inject_ref[side] = jnp.where(chip_plane == 0, done[side][3], done[2 + side][3])
    rank = jnp.minimum(lane // PER_SIDE, CHIP_BLOCKS)
    for (plane, side), state in zip(sims, done):
        hops = (travels[plane][side] >> (4 * rank)) & 15
        last = jnp.maximum(last, jnp.where(rank < totals[plane], state[2] + LAG * (hops - 1), 0))
    need = jnp.max(last) + 1
    variant = jnp.int32(0)
    for steps in STEPS[:-1]:
        variant = variant + flag(need > steps)
    wide_variant = jnp.int32(WIDE_FROM)
    for steps in WIDE_STEPS[:-1]:
        wide_variant = wide_variant + flag(need > steps)
    info_ref[VARIANT_AT] = jnp.where(wide == 1, wide_variant, variant)


def plan(occ_irrep, vir_irrep, pair_tiles, spin_mask):
    small = jnp.concatenate(
        [pair_tiles.reshape(-1), spin_mask.reshape(-1), occ_irrep, vir_irrep]
    )
    table = jax.ShapeDtypeStruct((2, RING, LANES), jnp.int32)
    return pl.pallas_call(
        plan_kernel,
        out_shape=(table, table, jax.ShapeDtypeStruct((INFO,), jnp.int32)),
        in_specs=[SMEM_SPEC],
        out_specs=(VMEM_SPEC, VMEM_SPEC, SMEM_SPEC),
        name="plan",
    )(small)


def ring_kernel(
    steps,
    cap,
    inject_ref,
    info_ref,
    amp_ref,
    int_ref,
    a_ref,
    b_ref,
    own,
    land,
    leave,
    *rest,
):
    if cap == 2:
        amp_own, amp_out = rest[:2]
        rest = rest[2:]
        amp_in = rest[0]
        rest = rest[1:]
    own_in, own_send, own_recv, send, recv, kept, f_send, f_recv, a_send, a_recv = rest
    o = lax.axis_index("occ")
    v = lax.axis_index("vir")
    core = v % 2
    mate = v + 1 - 2 * core
    across = (v + 2) % 4
    pos = ring_pos(o)
    right = ring_place((pos + 1) % RING)
    left = ring_place((pos + RING - 1) % RING)
    half = SQUARE // 2
    a_total = cap * A_PARTS

    def own_rows(k, side, group):
        rows = PER_SIDE * PIECE // GROUPS
        start = side * PER_SIDE * PIECE + group * rows
        to = own.at[pl.ds(pl.multiple_of((2 * core + k) * half + start, rows), rows)]

        def source(which):
            row = pl.multiple_of(which * half + start, rows)
            return int_ref.at[pl.ds(row, rows), pl.ds(k * SQUARE, SQUARE)]

        stay = pltpu.make_async_copy(source(core), to, own_in.at[k, side, group])
        give = pltpu.make_async_remote_copy(
            src_ref=source(1 - core),
            dst_ref=to,
            send_sem=own_send.at[k, side, group],
            recv_sem=own_recv.at[k, side, group],
            device_id=(o, mate),
            device_id_type=MESH,
        )
        return stay, give

    def own_parts(group):
        return [own_rows(k, side, group) for k in range(2) for side in range(2)]

    def amp_copy(k):
        return pltpu.make_async_copy(
            amp_ref.at[pl.ds(k // 2 * SQUARE, SQUARE), pl.ds(k % 2 * SQUARE, SQUARE)],
            amp_own.at[k],
            amp_in.at[k],
        )

    for group in range(GROUPS):
        for stay, _ in own_parts(group):
            stay.start()
    if cap == 2:
        for k in range(4):
            amp_copy(k).start()

    barrier = pltpu.get_barrier_semaphore()
    for target in ((right, v), (left, v), (o, mate), (o, across)):
        pl.semaphore_signal(barrier, inc=1, device_id=target, device_id_type=MESH)
    pl.semaphore_wait(barrier, 4)

    for group in range(GROUPS):
        for _, give in own_parts(group):
            give.start()

    def a_copy(which, index):
        slot = index // A_PARTS
        rows = SQUARE // A_PARTS
        cut = pl.ds(pl.multiple_of(index % A_PARTS * rows, rows), rows)
        owner = across if which == 2 else v
        if which == 2:
            source = a_ref.at[owner, slot, cut]
        elif cap == 2:
            source = amp_out.at[slot, cut]
        else:
            start = pl.multiple_of(slot // 2 * SQUARE + index % A_PARTS * rows, rows)
            source = amp_ref.at[
                pl.ds(start, rows), pl.ds(pl.multiple_of(slot % 2 * SQUARE, SQUARE), SQUARE)
            ]
        return pltpu.make_async_remote_copy(
            src_ref=source,
            dst_ref=a_ref.at[owner, slot, cut],
            send_sem=a_send.at[which, index],
            recv_sem=a_recv.at[which, index],
            device_id=(o, across if which == 0 else mate),
            device_id_type=MESH,
        )

    def hop(side, tau):
        return pltpu.make_async_remote_copy(
            src_ref=leave.at[side, tau % SLOTS],
            dst_ref=land.at[side, tau],
            send_sem=send.at[side, tau % SLOTS],
            recv_sem=recv.at[side, tau],
            device_id=(right if side == 0 else left, v),
            device_id_type=MESH,
        )

    def compose(side, tau, forward):
        p = tau % PER_SIDE
        block = (inject_ref[side, pos, tau // PER_SIDE] >> (4 * p)) & 15
        pieces = []
        for k in range(CHIP_BLOCKS):
            row = ((2 * k + side) * PER_SIDE + p) * PIECE
            pieces.append(own[pl.ds(pl.multiple_of(row, PIECE), PIECE), :])
        value = land[side, tau - LAG] if forward else pieces[0]
        for k in range(CHIP_BLOCKS):
            value = jnp.where(block == k + 1, pieces[k], value)
        leave[side, tau % SLOTS] = value

    def pass_on(start, size, side):
        cut = pl.ds(start, size)
        stay = pltpu.make_async_copy(land.at[side, cut], b_ref.at[core, side, cut], kept)
        give = pltpu.make_async_remote_copy(
            src_ref=land.at[side, cut],
            dst_ref=b_ref.at[core, side, cut],
            send_sem=f_send,
            recv_sem=f_recv,
            device_id=(o, mate),
            device_id_type=MESH,
        )
        return stay, give

    def amp_start(slot):
        if cap == 2:
            pick = jnp.where(slot == 0, info_ref[SLOT_AT], info_ref[SLOT_AT + 1])

            @pl.loop(0, SQUARE // 64)
            def _(part):
                cut = pl.ds(pl.multiple_of(part * 64, 64), 64)
                value = amp_own[0, cut]
                for k in range(1, 4):
                    value = jnp.where(pick == k, amp_own[k, cut], value)
                amp_out[slot, cut] = value

        for part in range(A_PARTS):
            for which in range(2):
                a_copy(which, slot * A_PARTS + part).start()

    def amp_forward(index):
        a_copy(0, index).wait_recv()
        a_copy(2, index).start()

    def hand_over(start):
        for side in range(2):
            for copy in pass_on(start, BATCH, side):
                copy.start()

    def own_wait(tau):
        @pl.when((tau < PER_SIDE) & (tau % (PER_SIDE // GROUPS) == 0))
        def _():
            for stay, give in own_parts(tau // (PER_SIDE // GROUPS)):
                stay.wait()
                give.wait_recv()

    @pl.loop(0, LAG)
    def _(tau):
        own_wait(tau)
        for side in range(2):
            compose(side, tau, False)
            hop(side, tau).start()

    if cap == 2:
        for k in range(4):
            amp_copy(k).wait()

    @pl.loop(LAG, steps)
    def _(tau):
        own_wait(tau)
        for side in range(2):
            hop(side, tau - LAG).wait_recv()

            @pl.when(tau >= SLOTS)
            def _():
                hop(side, tau - SLOTS).wait_send()

            compose(side, tau, True)
            hop(side, tau).start()

        @pl.when((tau >= BATCH + LAG - 1) & (tau % BATCH == (LAG - 1) % BATCH))
        def _():
            hand_over(tau - (BATCH + LAG - 1))

        @pl.when((tau % 2 == LAG % 2) & (tau < LAG + 2 * cap))
        def _():
            amp_start((tau - LAG) // 2)

        late = tau // PER_SIDE - A_LATE

        @pl.when((tau % PER_SIDE == 0) & (late >= 0) & (late < a_total))
        def _():
            amp_forward(late)

    done = min(max((steps - 1) // PER_SIDE - A_LATE + 1, 0), a_total)

    @pl.loop(done, a_total)
    def _(index):
        amp_forward(index)

    @pl.loop(steps - LAG, steps)
    def _(tau):
        for side in range(2):
            hop(side, tau).wait_recv()

    hand_over(steps - BATCH)

    @pl.loop(steps - SLOTS, steps)
    def _(tau):
        for side in range(2):
            hop(side, tau).wait_send()

    @pl.loop(0, GROUPS)
    def _(group):
        for _, give in own_parts(group):
            give.wait_send()

    @pl.loop(0, a_total)
    def _(index):
        for which in range(3):
            copy = a_copy(which, index)
            copy.wait_send()
            if which > 0:
                copy.wait_recv()

    every = pl.ds(0, steps)
    pltpu.make_async_copy(land, b_ref.at[core, :, every], kept).wait()
    total = pltpu.make_async_remote_copy(
        src_ref=land,
        dst_ref=b_ref.at[1 - core, :, every],
        send_sem=f_send,
        recv_sem=f_recv,
        device_id=(o, mate),
        device_id_type=MESH,
    )
    total.wait_send()
    total.wait_recv()


def ring(which, steps, cap, inject, info, amplitudes, integrals):
    square = (SQUARE, SQUARE)
    dma = pltpu.SemaphoreType.DMA
    kind = amplitudes.dtype
    amp_scratch = []
    if cap == 2:
        amp_scratch = [
            pltpu.VMEM((4,) + square, kind),
            pltpu.VMEM((2,) + square, kind),
            dma((4,)),
        ]
    return pl.pallas_call(
        functools.partial(ring_kernel, steps, cap),
        out_shape=(
            jax.ShapeDtypeStruct((4, 4) + square, kind),
            jax.ShapeDtypeStruct((2, 2, SPAN, PIECE, SQUARE), kind),
        ),
        in_specs=[SMEM_SPEC, SMEM_SPEC, ANY_SPEC, ANY_SPEC],
        out_specs=(ANY_SPEC, ANY_SPEC),
        scratch_shapes=[
            pltpu.VMEM((2 * SQUARE, SQUARE), kind),
            pltpu.VMEM((2, steps, PIECE, SQUARE), kind),
            pltpu.VMEM((2, SLOTS, PIECE, SQUARE), kind),
        ]
        + amp_scratch
        + [
            dma((2, 2, GROUPS)),
            dma((2, 2, GROUPS)),
            dma((2, 2, GROUPS)),
            dma((2, SLOTS)),
            dma((2, steps)),
            dma,
            dma,
            dma,
            dma((3, cap * A_PARTS)),
            dma((3, cap * A_PARTS)),
        ],
        compiler_params=pltpu.CompilerParams(
            collective_id=which, has_side_effects=True, vmem_limit_bytes=58 << 20
        ),
        name="ring",
    )(inject, info, amplitudes, integrals)


def ladder_kernel(
    info_ref,
    when_ref,
    occ_ref,
    vir_ref,
    amp_ref,
    int_ref,
    a_ref,
    b_ref,
    other_ref,
    out_ref,
    terms,
    a_buf,
    b_buf,
    other_buf,
    acc,
    result,
    blank,
    a_sem,
    b_sem,
    other_sem,
    out_sem,
    blank_sem,
):
    o = lax.axis_index("occ")
    v = lax.axis_index("vir")
    pos = ring_pos(o)
    wide = info_ref[WIDE_AT]
    rows = [info_ref[ROW_AT + 2 * o + r] for r in range(2)]

    def out_block(ref, b):
        return ref.at[
            pl.ds(pl.multiple_of(b // 2 * SQUARE, SQUARE), SQUARE),
            pl.ds(pl.multiple_of(b % 2 * SQUARE, SQUARE), SQUARE),
        ]

    def keep(b):
        return ((rows[b // 2] >> (2 * v + b % 2)) & 1) == 1

    count = jnp.int32(0)
    for b in range(4):
        alive = jnp.where(keep(b), 1, 0)
        for s in range(8):
            bit = alive * ((rows[b // 2] >> s) & 1)

            @pl.when(bit == 1)
            def _():
                terms[count] = b * 8 + s

            count = count + bit
    terms[count] = 64

    def fetch(j, slot):
        code = terms[j]
        b = code // 8
        s = code % 8
        r = b // 2
        tile = 2 * (v % 2) + b % 2
        src = s // 2
        block = r * 2 + s % 2

        @pl.when(src == v)
        def _():
            pltpu.make_async_copy(out_block(amp_ref, block), a_buf.at[slot], a_sem.at[slot]).start()

        @pl.when(src != v)
        def _():
            low = (rows[0] >> (2 * src)) & 3
            high = (rows[1] >> (2 * src)) & 3
            flags = low | (high << 2)
            below = flags & ((1 << block) - 1)
            rank = (below & 1) + ((below >> 1) & 1) + ((below >> 2) & 1)
            at = jnp.where(wide == 1, block, rank)
            pltpu.make_async_copy(a_ref.at[src, at], a_buf.at[slot], a_sem.at[slot]).start()

        @pl.when(s == o)
        def _():
            cols = pl.ds(pl.multiple_of(b % 2 * SQUARE, SQUARE), SQUARE)
            for k in range(2 * 2 * PER_SIDE):
                pltpu.make_async_copy(
                    int_ref.at[pl.ds(k * PIECE, PIECE), cols],
                    b_buf.at[slot, k // (2 * PER_SIDE), k // PER_SIDE % 2, k % PER_SIDE],
                    b_sem.at[slot],
                ).start()

        @pl.when(s != o)
        def _():
            flags = (info_ref[SENT_AT + s] >> (CHIP_BLOCKS * (v // 2))) & 15
            below = flags & ((1 << tile) - 1)
            rank = (below & 1) + ((below >> 1) & 1) + ((below >> 2) & 1)
            owner = ring_pos(s)
            for side in range(2):
                away = (pos - owner if side == 0 else owner - pos) % RING
                for p in range(PER_SIDE):
                    start = when_ref[side, owner, rank * PER_SIDE + p]
                    step = start + LAG * (away - 1)
                    pltpu.make_async_copy(
                        b_ref.at[:, side, step],
                        b_buf.at[slot, :, side, p],
                        b_sem.at[slot],
                    ).start()

    @pl.when(count > 0)
    def _():
        fetch(0, 0)

    def other_copy(b):
        return pltpu.make_async_copy(out_block(other_ref, b), other_buf.at[b], other_sem.at[b])

    def blank_copy(b):
        return pltpu.make_async_copy(blank, out_block(out_ref, b), blank_sem.at[b])

    for b in range(4):

        @pl.when(keep(b))
        def _():
            other_copy(b).start()

    blank[...] = jnp.zeros_like(blank)
    for b in range(4):

        @pl.when(jnp.logical_not(keep(b)))
        def _():
            blank_copy(b).start()

    def out_copy(b):
        return pltpu.make_async_copy(result.at[b % 2], out_block(out_ref, b), out_sem.at[b % 2])

    @pl.loop(0, count, init_carry=(jnp.int32(-1), jnp.int32(-1)))
    def last_out(j, carry):
        slot = j % 2

        @pl.when(j + 1 < count)
        def _():
            fetch(j + 1, 1 - slot)

        code = terms[j]
        b = code // 8
        before = jnp.where(j == 0, -1, terms[jnp.maximum(j - 1, 0)] // 8)
        fresh = before != b
        final = terms[j + 1] // 8 != b
        pltpu.make_async_copy(out_block(amp_ref, 0), a_buf.at[slot], a_sem.at[slot]).wait()
        pltpu.make_async_copy(b_buf.at[slot], b_buf.at[slot], b_sem.at[slot]).wait()

        def product(part):
            cols = pl.ds(pl.multiple_of(part * STEP_COLS, STEP_COLS), STEP_COLS)
            right = b_buf[slot, :, :, :, :, cols].reshape(SQUARE, STEP_COLS)
            return cols, jnp.dot(a_buf[slot], right, preferred_element_type=jnp.float32)

        @pl.when(fresh)
        def _():
            acc[...] = jnp.zeros_like(acc)

        @pl.when(jnp.logical_not(final))
        def _():
            @pl.loop(0, SQUARE // STEP_COLS)
            def _(part):
                cols, term = product(part)
                acc[:, cols] += term

        @pl.when(final)
        def _():
            other_copy(b).wait()
            pending = jnp.where(b % 2 == 0, carry[0], carry[1])

            @pl.when(pending >= 0)
            def _():
                out_copy(b).wait()

            @pl.loop(0, SQUARE // STEP_COLS)
            def _(part):
                cols, term = product(part)
                denom = occ_ref[b // 2] - vir_ref[b % 2, :, cols]
                total = (acc[:, cols] + term) + other_buf[b, :, cols].astype(jnp.float32)
                result[b % 2, :, cols] = (total / denom).astype(result.dtype)

            out_copy(b).start()

        even = jnp.where(final & (b % 2 == 0), b, carry[0])
        odd = jnp.where(final & (b % 2 == 1), b, carry[1])
        return even, odd

    for k in range(2):

        @pl.when(last_out[k] >= 0)
        def _():
            out_copy(k).wait()

    for b in range(4):

        @pl.when(jnp.logical_not(keep(b)))
        def _():
            blank_copy(b).wait()


def ladder(info, when, occ_sum, vir_sum, amplitudes, integrals, a_all, b_all, other_terms):
    square = (SQUARE, SQUARE)
    kind = amplitudes.dtype
    dma = pltpu.SemaphoreType.DMA
    return pl.pallas_call(
        ladder_kernel,
        out_shape=jax.ShapeDtypeStruct(other_terms.shape, other_terms.dtype),
        in_specs=[SMEM_SPEC, SMEM_SPEC, VMEM_SPEC, VMEM_SPEC] + [ANY_SPEC] * 5,
        out_specs=ANY_SPEC,
        scratch_shapes=[
            pltpu.SMEM((40,), jnp.int32),
            pltpu.VMEM((2,) + square, kind),
            pltpu.VMEM((2, 2, 2, PER_SIDE, PIECE, SQUARE), kind),
            pltpu.VMEM((4,) + square, kind),
            pltpu.VMEM(square, jnp.float32),
            pltpu.VMEM((2,) + square, kind),
            pltpu.VMEM(square, kind),
            dma((2,)),
            dma((2,)),
            dma((4,)),
            dma((2,)),
            dma((4,)),
        ],
        compiler_params=pltpu.CompilerParams(vmem_limit_bytes=48 << 20),
        name="ladder",
    )(info, when, occ_sum, vir_sum, amplitudes, integrals, a_all, b_all, other_terms)


def block_device(
    amplitudes,
    integrals,
    other_terms,
    occ_irrep,
    vir_irrep,
    pair_tiles,
    spin_mask,
    occ_energy,
    vir_energy,
):
    o = lax.axis_index("occ")
    v = lax.axis_index("vir")
    occ_tiles = occ_energy.reshape(OTILES, TILE)
    pair_occ = (occ_tiles[:, None, :, None] + occ_tiles[None, :, None, :]).reshape(-1, SQUARE)
    occ_sum = lax.dynamic_slice_in_dim(pair_occ, 2 * o, 2, 0)[:, :, None]
    vir_tiles = vir_energy.reshape(-1, TILE)
    tiles = lax.dynamic_slice_in_dim(pair_tiles, 2 * v, 2, 0)
    first = lookup(tiles[:, 0], vir_tiles)
    second = lookup(tiles[:, 1], vir_tiles)
    vir_sum = (first[:, :, None] + second[:, None, :]).reshape(2, 1, SQUARE)

    inject, when, info = plan(occ_irrep, vir_irrep, pair_tiles, spin_mask)
    inject, when, info, occ_sum, vir_sum = lax.optimization_barrier(
        (inject, when, info, occ_sum, vir_sum)
    )
    branches = [functools.partial(ring, k, steps, 2) for k, steps in enumerate(STEPS)]
    branches += [
        functools.partial(ring, WIDE_FROM + k, steps, 4) for k, steps in enumerate(WIDE_STEPS)
    ]
    a_all, b_all = lax.switch(
        info[VARIANT_AT], branches, inject, info, amplitudes, integrals
    )
    return ladder(info, when, occ_sum, vir_sum, amplitudes, integrals, a_all, b_all, other_terms)


def per_device(amplitudes, integrals, *rest):
    blocks = amplitudes.shape == (2 * SQUARE, 2 * SQUARE)
    blocks = blocks and integrals.shape == (SQUARE, 2 * SQUARE) and lax.axis_size("vir") == 4
    blocks = blocks and lax.axis_size("occ") == OTILES * OTILES // 2
    device = block_device if blocks else dense_device
    return device(amplitudes, integrals, *rest)


def solution(mesh):
    in_specs = (P("occ", "vir"), P("occ", "vir"), P("occ", "vir"), P(), P(), P(), P(), P(), P())
    out_specs = P("occ", "vir")
    return jax.shard_map(
        per_device, mesh=mesh, in_specs=in_specs, out_specs=out_specs, check_vma=False
    )
```
